256 devices in a mesh: dp: 2 (over core), row: 16 (over y, x), col: 8 (over z).
Axes of the slice: x: 4, y: 4, z: 8, core: 2. Of those that a mesh axis runs over, the one named last changes fastest.
Arguments:
- states: bfloat16 [12288, 4096], P(('dp', 'row'), 'col'), may hold values from -6 to 6
- actions: bfloat16 [12288, 24], P(('dp', 'row')), may hold values from -6 to 6
- rewards: float32 [12288], P(('dp', 'row')), may hold values from -6 to 6
- terminal: int32 [12288], P(('dp', 'row')), may hold values 0 or 1
- next_index: int32 [12288], P(('dp', 'row')), may hold values from 0 to 12287
- hidden_weights: bfloat16 [4, 4096, 4096], P(None, 'col', 'row'), may hold values from -0.09375 to 0.09375
- action_weights: bfloat16 [2, 24, 4096], replicated, may hold values from -1.25 to 1.25
- heads: bfloat16 [4096, 27], replicated, may hold values from -0.09375 to 0.09375
- policy_scale: float32 [24], replicated, may hold values from 0.5 to 2
Outputs:
- advantage: float32 [12288], P(('dp', 'row'))
- losses: float32 [3], replicated
- head_grads: float32 [4096, 27], replicated
The draws below stay inside these ranges and needn't reach their ends.
Inputs may be any that keep to these rules, and one draw needn't show every extreme that they name: `next_index`: any batch row, from any device.
All inputs are finite; a program needn't handle non-finite values. No bound on the sum of `terminal` on one device may be relied on, other than what follows from the above.
Results may differ from the reference program's by a relative error of at most 0.0038.
Values may be sent and summed in bfloat16 or wider, within the bound.
A program may use at most 128 MiB of HBM per device.

```python
import math
import jax
import jax.numpy as jnp
from jax import lax

D = 4096
ACT = 24
TOKENS = 12288


def with_ends(result, rng, smallest, high):
    place = [jax.random.randint(jax.random.fold_in(rng, axis), (), 0, length) for axis, length in enumerate(result.shape)]
    longest = result.shape.index(max(result.shape))
    beside = place[:longest] + [(place[longest] + 1) % result.shape[longest]] + place[longest + 1:]
    return result.at[tuple(place)].set(smallest).at[tuple(beside)].set(high)


def steps_of(rng, shape, shards, low, top_value):
    def one(dim, blocks):
        draws = jax.random.uniform(jax.random.fold_in(jax.random.fold_in(rng, 6), dim), (blocks,), jnp.float32, low / len(shards), top_value / len(shards))
        return jnp.repeat(jnp.exp(draws), shape[dim] // blocks).reshape((-1,) + (1,) * (len(shape) - dim - 1))

    factor_of = one(*shards[0])
    for cut in shards[1:]:
        factor_of = factor_of * one(*cut)
    return factor_of


def gaussian(own_key, extent, scale, reach, split=(), held_as=jnp.bfloat16):
    values = jax.random.normal(own_key, extent, jnp.float32) * scale
    if len(split) > 0:
        values = steps_of(own_key, extent, split, -0.22, 0.18) * values
    return jnp.clip(values, min=-reach, max=reach).astype(held_as)


def setup_inputs(seed: int = 0) -> dict:
    seeds = jax.random.split(jax.random.key(seed), 10)
    states = gaussian(seeds[0], (TOKENS, D), 1.0, 6.0, ((0, 32), (1, 8)))
    actions = gaussian(seeds[1], (TOKENS, ACT), 1.0, 6.0, ((0, 32),))
    rewards = gaussian(seeds[2], (TOKENS,), 1.0, 6.0, ((0, 32),), jnp.float32)
    terminal = with_ends((jax.random.randint(seeds[3], (TOKENS,), 0, 8) < 1).astype(jnp.int32), jax.random.fold_in(seeds[3], 1), 0, 1)
    next_index = with_ends(jax.random.randint(seeds[4], (TOKENS,), 0, TOKENS), jax.random.fold_in(seeds[4], 1), 0, TOKENS - 1).astype(jnp.int32)
    hidden_weights = gaussian(seeds[5], (4, D, D), D ** -0.5, 0.09375, ((1, 8), (2, 16)))
    action_weights = gaussian(seeds[6], (2, ACT, D), ACT ** -0.5, 1.25)
    heads = gaussian(seeds[7], (D, 3 + ACT), D ** -0.5, 0.09375)
    policy_scale = jnp.clip(jnp.exp(jax.random.uniform(seeds[8], (ACT,), jnp.float32, math.log(0.5), math.log(2.0))), 0.5, 2.0)
    return {"states": states, "actions": actions, "rewards": rewards, "terminal": terminal, "next_index": next_index, "hidden_weights": hidden_weights, "action_weights": action_weights, "heads": heads, "policy_scale": policy_scale}


GAMMA = 0.99
TAU = 0.7
FLOOR = 0.01

def reference(states, actions, rewards, terminal, next_index, hidden_weights, action_weights, heads, policy_scale):
    hidden = []
    for network in range(4):
        pre = jnp.dot(states, hidden_weights[network], preferred_element_type=jnp.float32)
        if network < 2:
            pre = pre + jnp.dot(actions, action_weights[network], preferred_element_type=jnp.float32)
        hidden.append(jnp.maximum(pre, 0.0).astype(jnp.bfloat16))
    first_q = jnp.dot(hidden[0], heads[:, 0], preferred_element_type=jnp.float32)
    second_q = jnp.dot(hidden[1], heads[:, 1], preferred_element_type=jnp.float32)
    value = jnp.dot(hidden[2], heads[:, 2], preferred_element_type=jnp.float32)
    policy_mean = jnp.dot(hidden[3], heads[:, 3:], preferred_element_type=jnp.float32)
    advantage = jnp.minimum(first_q, second_q) - value
    target = rewards + GAMMA * (1.0 - terminal.astype(jnp.float32)) * value[next_index.astype(jnp.int32)]
    top = jnp.max(advantage)
    weight = jnp.maximum(jnp.exp(advantage - top), FLOOR)
    expectile = jnp.where(advantage >= 0.0, TAU, 1.0 - TAU)
    scaled = (actions.astype(jnp.float32) - policy_mean) / policy_scale
    log_prob = -0.5 * lax.optimization_barrier(jnp.sum(scaled * scaled, axis=1))
    losses = jnp.stack([jnp.sum(expectile * advantage * advantage), jnp.sum((first_q - target) ** 2 + (second_q - target) ** 2), -jnp.sum(weight * log_prob)]) / TOKENS
    coeff_policy = -weight[:, None] * scaled / policy_scale
    columns = [(hidden[0], (2.0 * (first_q - target))[:, None]), (hidden[1], (2.0 * (second_q - target))[:, None]), (hidden[2], (-2.0 * expectile * advantage)[:, None]), (hidden[3], coeff_policy)]
    grads = jnp.concatenate([jnp.dot(units.astype(jnp.float32).T, coeff, precision=lax.Precision.HIGHEST) for units, coeff in columns], axis=1)
    return (advantage, losses, grads / jnp.sqrt(jnp.float32(TOKENS)))
```

```python
import functools
import math

import jax
import jax.numpy as jnp
from jax import lax
from jax.experimental import pallas as pl
from jax.experimental.pallas import tpu as pltpu
from jax.sharding import PartitionSpec as P

D = 4096
ACT = 24
GAMMA = 0.99
TAU = 0.7
FLOOR = 0.01
MESH = pl.DeviceIdType.MESH
F32 = jnp.float32
BF16 = jnp.bfloat16

ORDER = (0, 1, 7, 2, 6, 3, 5, 4)


def place():
    row = lax.axis_index("row")
    return lax.axis_index("dp"), row // 4, row % 4, lax.axis_index("col")


def forward_kernel(
    states, weights, act_t, act_w, heads_t, hid, part,
    wa, wb, a, acc, local_sem, ss, rs,
):
    d, y, x, z = place()
    net, half = z // 2, z % 2

    def dev(dd=None, yy=None, xx=None, zz=None):
        yy = y if yy is None else yy
        xx = x if xx is None else xx
        return (d if dd is None else dd, yy * 4 + xx, z if zz is None else zz)

    peers = [dev(zz=(z + k) % 8) for k in range(1, 8)]
    peers += [dev(xx=(x + k) % 4) for k in range(1, 4)]
    peers += [dev(yy=(y + k) % 4) for k in range(1, 4)]
    peers += [dev(dd=1 - d)]

    own = [
        pltpu.make_async_copy(
            weights.at[net, pl.ds(d * 256 + 128 * i, 128), pl.ds(half * 128, 128)],
            dst, local_sem.at[i],
        )
        for i, dst in enumerate((wa.at[z, d, y, x], wb.at[z, d, x, y]))
    ]
    own_states = pltpu.make_async_copy(states, a.at[z], local_sem.at[2])
    for c in own:
        c.start()
    own_states.start()

    barrier = pltpu.get_barrier_semaphore()
    for p in peers:
        pl.semaphore_signal(barrier, inc=1, device_id=p, device_id_type=MESH)
    pl.semaphore_wait(barrier, len(peers))

    used = [0]
    sent = []

    def send(src, dst, device):
        i = used[0]
        used[0] += 1
        c = pltpu.make_async_remote_copy(
            src_ref=src, dst_ref=dst, send_sem=ss.at[i], recv_sem=rs.at[i],
            device_id=device, device_id_type=MESH,
        )
        c.start()
        sent.append(c)
        return c

    def drain(keep):
        while len(sent) > keep:
            sent.pop(0).wait_send()

    scatter = {}

    def scatter_weights(k):
        zt = (z + k) % 8
        cols = pl.ds(pl.multiple_of((zt % 2) * 128, 128), 128)
        scatter[(8 - k) % 8] = [
            send(
                weights.at[zt // 2, pl.ds(pl.multiple_of(d * 256 + 128 * i, 128), 128), cols],
                dst, dev(zz=zt),
            )
            for i, dst in enumerate((wa.at[z, d, y, x], wb.at[z, d, x, y]))
        ]

    state_step = {}

    def send_states(t):
        copies = []
        for sign in (1, -1):
            c = (z - sign * (t - 1)) % 8
            pieces = (0, 1) if t < 4 else ((0,) if sign == 1 else (1,))
            for p in pieces:
                rows = pl.ds(p * 192, 192)
                src = states.at[rows] if t == 1 else a.at[c, rows]
                copies.append(send(src, a.at[c, rows], dev(zz=(z + sign) % 8)))
        state_step[t] = copies

    def wait_all(copies):
        for c in copies:
            c.wait_recv()

    first, second, swap = {}, {}, {}

    def gather_first(r):
        c = (z + r) % 8
        first[r] = []
        for k in (1, 3, 2):
            w = wa.at[c, d, y, x]
            first[r].append(send(w, w, dev(xx=(x + k) % 4)))
            w = wb.at[c, d, x, y]
            first[r].append(send(w, w, dev(yy=(y + k) % 4)))

    def gather_second(r):
        wait_all(first[r])
        c = (z + r) % 8
        second[r] = []
        for k in (1, 3, 2):
            w = wa.at[c, d, y]
            second[r].append(send(w, w, dev(yy=(y + k) % 4)))
            w = wb.at[c, d, x]
            second[r].append(send(w, w, dev(xx=(x + k) % 4)))

    def exchange(r):
        wait_all(second[r])
        c = (z + r) % 8
        swap[r] = [send(w, w, dev(dd=1 - d)) for w in (wa.at[c, d], wb.at[c, d])]

    def product(r):
        wait_all(swap[r])
        c = (z + r) % 8

        def tile(j, _):
            yy, x0 = j // 2, 2 * (j % 2)
            rows = []
            for dd in (0, 1):
                rows.append(jnp.concatenate([wa[c, dd, yy, x0], wa[c, dd, yy, x0 + 1]], axis=1))
                rows.append(jnp.concatenate([wb[c, dd, x0, yy], wb[c, dd, x0 + 1, yy]], axis=1))
            w = jnp.concatenate(rows, axis=0)
            acc[j] += jnp.dot(a[c], w, preferred_element_type=F32)
            return 0

        lax.fori_loop(0, 8, tile, 0)

    scatter_weights(1)
    scatter_weights(7)
    for c in own:
        c.wait()
    gather_first(0)
    send_states(1)
    for k in (2, 6, 3, 5, 4):
        scatter_weights(k)

    weight_net = jnp.minimum(net, 1)
    gate = jnp.where(net < 2, 1.0, 0.0)
    act = act_t[...]

    def start_tile(j, _):
        cols = [
            act_w[weight_net, :, pl.ds(pl.multiple_of((2 * j + i) * 256 + half * 128, 128), 128)]
            for i in (0, 1)
        ]
        share = lax.dot_general(
            act, jnp.concatenate(cols, axis=1), (((0,), (0,)), ((), ())),
            preferred_element_type=F32,
        )
        acc[j] = share * gate
        return 0

    wait_all(scatter[1])
    gather_first(1)
    gather_second(0)
    lax.fori_loop(0, 8, start_tile, 0)
    own_states.wait()

    after = {1: [0], 3: [1, 7], 5: [2, 6]}
    for i, r in enumerate(ORDER):
        if i + 2 < 8:
            wait_all(scatter[ORDER[i + 2]])
            gather_first(ORDER[i + 2])
        if i + 1 < 8:
            gather_second(ORDER[i + 1])
        exchange(r)
        if i in (1, 3, 5):
            t = (i + 1) // 2
            wait_all(state_step[t])
            send_states(t + 1)
        for m in after.get(i, []):
            product(m)
        drain(60)
    product(3)
    product(5)
    wait_all(state_step[4])
    product(4)

    total = jnp.zeros((27, 384), F32)
    for j in range(8):
        h = jnp.maximum(acc[j], 0.0).astype(BF16)
        hid[j] = h
        cols = [
            heads_t[:, pl.ds(pl.multiple_of((2 * j + i) * 256 + half * 128, 128), 128)]
            for i in (0, 1)
        ]
        total += lax.dot_general(
            jnp.concatenate(cols, axis=1), h, (((1,), (1,)), ((), ())),
            preferred_element_type=F32,
        )
    mine = jnp.minimum(lax.broadcasted_iota(jnp.int32, (27, 384), 0), 3) == net
    part[...] = jnp.where(mine, total, 0.0)
    drain(0)


N_COPIES = 14 + 14 + 48 + 48 + 16


def forward(states, weights, act_t, act_w, heads_t):
    vmem = pl.BlockSpec(memory_space=pltpu.VMEM)
    hbm = pl.BlockSpec(memory_space=pl.ANY)
    return pl.pallas_call(
        forward_kernel,
        out_shape=(
            jax.ShapeDtypeStruct((8, 384, 256), BF16),
            jax.ShapeDtypeStruct((27, 384), F32),
        ),
        in_specs=[hbm, hbm, vmem, vmem, vmem],
        out_specs=(vmem, vmem),
        scratch_shapes=[
            pltpu.VMEM((8, 2, 4, 4, 128, 128), BF16),
            pltpu.VMEM((8, 2, 4, 4, 128, 128), BF16),
            pltpu.VMEM((8, 384, 512), BF16),
            pltpu.VMEM((8, 384, 256), F32),
            pltpu.SemaphoreType.DMA((3,)),
            pltpu.SemaphoreType.DMA((N_COPIES,)),
            pltpu.SemaphoreType.DMA((N_COPIES,)),
        ],
        compiler_params=pltpu.CompilerParams(
            collective_id=0, has_side_effects=True, vmem_limit_bytes=48 * 2**20
        ),
        name="forward",
    )(states, weights, act_t, act_w, heads_t)


def shards(states, actions, rewards, terminal, next_index, hidden_weights, action_weights, heads, policy_scale):
    total_rows = states.shape[0] * 32
    hid, part = forward(states, hidden_weights, actions.T, action_weights, heads.T)
    net, half = lax.axis_index("col") // 2, lax.axis_index("col") % 2
    full = lax.psum(part, "col")
    first_q, second_q, value, policy_mean = full[0], full[1], full[2], full[3:]
    advantage = jnp.minimum(first_q, second_q) - value
    value_whole = lax.all_gather(value, ("dp", "row"), tiled=True)
    top = lax.pmax(jnp.max(advantage), ("dp", "row"))
    target = rewards + GAMMA * (1.0 - terminal.astype(F32)) * jnp.take(value_whole, next_index, axis=0)
    weight = jnp.maximum(jnp.exp(advantage - top), FLOOR)
    expectile = jnp.where(advantage >= 0.0, TAU, 1.0 - TAU)
    scaled = (actions.T.astype(F32) - policy_mean) / policy_scale[:, None]
    log_prob = -0.5 * jnp.sum(scaled * scaled, axis=0)
    losses = jnp.stack([
        jnp.sum(expectile * advantage * advantage),
        jnp.sum((first_q - target) ** 2 + (second_q - target) ** 2),
        jnp.sum(-weight * log_prob),
    ])
    coeff = jnp.concatenate([
        jnp.stack([2.0 * (first_q - target), 2.0 * (second_q - target), -2.0 * expectile * advantage]),
        -weight * scaled / policy_scale[:, None],
    ])
    mine = jnp.minimum(jnp.arange(27), 3)[:, None] == net
    coeff = jnp.where(mine, coeff, 0.0)
    grads = jnp.einsum("rb,jbu->rju", coeff, hid.astype(F32), precision=lax.Precision.HIGHEST)
    grads = grads.reshape(27, 16, 1, 128)
    spread = jnp.where((jnp.arange(2) == half)[None, None, :, None], grads, 0.0).reshape(27, 4096)
    spread = lax.psum(spread, ("dp", "row", "col"))
    losses = lax.psum(losses, ("dp", "row")) / total_rows
    return advantage, losses, spread.T / math.sqrt(total_rows)


def solution(mesh):
    rows = P(("dp", "row"))
    return jax.shard_map(
        shards,
        mesh=mesh,
        in_specs=(P(("dp", "row"), "col"), P(("dp", "row"), None), rows, rows, rows, P(None, "col", "row"), P(), P(), P()),
        out_specs=(rows, P(), P()),
        check_vma=False,
    )
```

```python
import functools
import math

import jax
import jax.numpy as jnp
from jax import lax
from jax.experimental import pallas as pl
from jax.experimental.pallas import tpu as pltpu
from jax.sharding import PartitionSpec as P

D = 4096
ACT = 24
GAMMA = 0.99
TAU = 0.7
FLOOR = 0.01
MESH = pl.DeviceIdType.MESH
F32 = jnp.float32
BF16 = jnp.bfloat16

ORDER = (0, 1, 7, 2, 6, 3, 5, 4)


def place():
    row = lax.axis_index("row")
    return lax.axis_index("dp"), row // 4, row % 4, lax.axis_index("col")


def update_kernel(
    states, weights, act_hbm, act_w_hbm, heads_hbm, rewards, terminal, next_index, scale,
    adv_out, loss_out, grad_out,
    wa, wb, a, acc, hid, act_t, act_w, heads_t, qs, pol, vt, gb, rb, zb, ob, local_sem, ss, rs,
):
    d, y, x, z = place()
    net, half = z // 2, z % 2

    def dev(dd=None, yy=None, xx=None, zz=None):
        yy = y if yy is None else yy
        xx = x if xx is None else xx
        return (d if dd is None else dd, yy * 4 + xx, z if zz is None else zz)

    line = [dev(zz=(z + k) % 8) for k in range(1, 8)]
    plane = [
        dev((d + dd) % 2, (y + ky) % 4, (x + kx) % 4)
        for ky in range(4) for kx in range(4) for dd in range(2) if ky or kx or dd
    ]
    peers = line + plane

    own = [
        pltpu.make_async_copy(
            weights.at[net, pl.ds(d * 256 + 128 * i, 128), pl.ds(half * 128, 128)],
            dst, local_sem.at[i],
        )
        for i, dst in enumerate((wa.at[z, d, y, x], wb.at[z, d, x, y]))
    ]
    own_states = pltpu.make_async_copy(states, a.at[z], local_sem.at[2])
    for c in own:
        c.start()
    own_states.start()
    small = [
        pltpu.make_async_copy(src, dst, local_sem.at[3 + i])
        for i, (src, dst) in enumerate(((act_hbm, act_t), (act_w_hbm, act_w), (heads_hbm, heads_t)))
    ]
    for c in small:
        c.start()

    barrier = pltpu.get_barrier_semaphore()
    for p in peers:
        pl.semaphore_signal(barrier, inc=1, device_id=p, device_id_type=MESH)
    pl.semaphore_wait(barrier, len(peers))

    used = [0]
    sent = []

    def send(src, dst, device):
        i = used[0]
        used[0] += 1
        c = pltpu.make_async_remote_copy(
            src_ref=src, dst_ref=dst, send_sem=ss.at[i], recv_sem=rs.at[i],
            device_id=device, device_id_type=MESH,
        )
        c.start()
        sent.append(c)
        return c

    def drain(keep):
        while len(sent) > keep:
            sent.pop(0).wait_send()

    scatter = {}

    def scatter_weights(k):
        zt = (z + k) % 8
        cols = pl.ds(pl.multiple_of((zt % 2) * 128, 128), 128)
        scatter[(8 - k) % 8] = [
            send(
                weights.at[zt // 2, pl.ds(pl.multiple_of(d * 256 + 128 * i, 128), 128), cols],
                dst, dev(zz=zt),
            )
            for i, dst in enumerate((wa.at[z, d, y, x], wb.at[z, d, x, y]))
        ]

    state_step = {}

    def send_states(t):
        copies = []
        for sign in (1, -1):
            c = (z - sign * (t - 1)) % 8
            pieces = (0, 1) if t < 4 else ((0,) if sign == 1 else (1,))
            for p in pieces:
                rows = pl.ds(p * 192, 192)
                src = states.at[rows] if t == 1 else a.at[c, rows]
                copies.append(send(src, a.at[c, rows], dev(zz=(z + sign) % 8)))
        state_step[t] = copies

    def wait_all(copies):
        for c in copies:
            c.wait_recv()

    first, second, swap = {}, {}, {}

    def gather_first(r):
        c = (z + r) % 8
        first[r] = []
        for k in (1, 3, 2):
            w = wa.at[c, d, y, x]
            first[r].append(send(w, w, dev(xx=(x + k) % 4)))
            w = wb.at[c, d, x, y]
            first[r].append(send(w, w, dev(yy=(y + k) % 4)))

    def gather_second(r):
        wait_all(first[r])
        c = (z + r) % 8
        second[r] = []
        for k in (1, 3, 2):
            w = wa.at[c, d, y]
            second[r].append(send(w, w, dev(yy=(y + k) % 4)))
            w = wb.at[c, d, x]
            second[r].append(send(w, w, dev(xx=(x + k) % 4)))

    def exchange(r):
        wait_all(second[r])
        c = (z + r) % 8
        swap[r] = [send(w, w, dev(dd=1 - d)) for w in (wa.at[c, d], wb.at[c, d])]

    def product(r):
        wait_all(swap[r])
        c = (z + r) % 8

        def tile(j, _):
            yy, x0 = j // 2, 2 * (j % 2)
            rows = []
            for dd in (0, 1):
                rows.append(jnp.concatenate([wa[c, dd, yy, x0], wa[c, dd, yy, x0 + 1]], axis=1))
                rows.append(jnp.concatenate([wb[c, dd, x0, yy], wb[c, dd, x0 + 1, yy]], axis=1))
            w = jnp.concatenate(rows, axis=0)
            acc[j] += jnp.dot(a[c], w, preferred_element_type=F32)
            return 0

        lax.fori_loop(0, 8, tile, 0)

    scatter_weights(1)
    scatter_weights(7)
    for c in own:
        c.wait()
    gather_first(0)
    send_states(1)
    for k in (2, 6, 3, 5, 4):
        scatter_weights(k)

    weight_net = jnp.minimum(net, 1)
    gate = jnp.where(net < 2, 1.0, 0.0)
    for c in small:
        c.wait()
    act = act_t[...]

    def start_tile(j, _):
        cols = [
            act_w[weight_net, :, pl.ds(pl.multiple_of((2 * j + i) * 256 + half * 128, 128), 128)]
            for i in (0, 1)
        ]
        share = lax.dot_general(
            act, jnp.concatenate(cols, axis=1), (((0,), (0,)), ((), ())),
            preferred_element_type=F32,
        )
        acc[j] = share * gate
        return 0

    wait_all(scatter[1])
    gather_first(1)
    gather_second(0)
    lax.fori_loop(0, 8, start_tile, 0)
    own_states.wait()

    after = {1: [0], 3: [1, 7], 5: [2, 6]}
    for i, r in enumerate(ORDER):
        if i + 2 < 8:
            wait_all(scatter[ORDER[i + 2]])
            gather_first(ORDER[i + 2])
        if i + 1 < 8:
            gather_second(ORDER[i + 1])
        exchange(r)
        if i in (1, 3, 5):
            t = (i + 1) // 2
            wait_all(state_step[t])
            send_states(t + 1)
        for m in after.get(i, []):
            product(m)
        drain(60)
    product(3)
    product(5)
    wait_all(state_step[4])
    product(4)

    total = jnp.zeros((27, 384), F32)
    for j in range(8):
        h = jnp.maximum(acc[j], 0.0).astype(BF16)
        hid[j] = h
        cols = [
            heads_t[:, pl.ds(pl.multiple_of((2 * j + i) * 256 + half * 128, 128), 128)]
            for i in (0, 1)
        ]
        total += lax.dot_general(
            jnp.concatenate(cols, axis=1), h, (((1,), (1,)), ((), ())),
            preferred_element_type=F32,
        )
    mine = jnp.minimum(lax.broadcasted_iota(jnp.int32, (27, 384), 0), 3) == net
    part = jnp.where(mine, total, 0.0)

    row = y * 4 + x
    me = d * 16 + row
    qs[z] = jnp.sum(part[0:3], axis=0, keepdims=True)
    pol[0] = part[3:27]
    copies = [send(pol.at[0], pol.at[1], dev(zz=z + 1 - 2 * half))]
    copies += [send(qs.at[z], qs.at[z], p) for p in line]
    index = next_index[...].reshape(1, 384)
    r = lax.broadcasted_iota(jnp.int32, (256, 384), 0)
    block = jnp.where((r & 7) < 3, (r >> 3) * 3 + (r & 7), -1)
    pick = jnp.where(block == (index >> 7), 1.0, 0.0).astype(BF16)
    lane = lax.broadcasted_iota(jnp.int32, (128, 384), 0) == (index & 127)
    eye = lax.broadcasted_iota(jnp.int32, (24, 24), 0) == lax.broadcasted_iota(jnp.int32, (24, 24), 1)
    sigma = jnp.sum(jnp.where(eye, scale[...].reshape(1, 24), 0.0), axis=1, keepdims=True)
    wait_all(copies)
    first_q, second_q, value = qs[0] + qs[1], qs[2] + qs[3], qs[4] + qs[5]
    policy_mean = pol[0] + pol[1]
    advantage = jnp.minimum(first_q, second_q) - value
    vt[me] = jnp.concatenate(
        [value[:, 0:128], value[:, 128:256], value[:, 256:384],
         jnp.broadcast_to(jnp.max(advantage, axis=1, keepdims=True), (1, 128)), jnp.zeros((4, 128), F32)],
        axis=0,
    )
    copies = [send(vt.at[me], vt.at[me], p) for p in plane]
    adv_out[...] = advantage.reshape(384)
    expectile = jnp.where(advantage >= 0.0, TAU, 1.0 - TAU)
    scaled = (act_t[...].astype(F32) - policy_mean) / sigma
    log_prob = -0.5 * jnp.sum(scaled * scaled, axis=0, keepdims=True)
    wait_all(copies)

    table = vt[...].reshape(256, 128)
    fourth = (lax.broadcasted_iota(jnp.int32, (256, 128), 0) & 7) == 3
    top = jnp.max(jnp.where(fourth, table, -jnp.inf), keepdims=True)
    table = table.T
    high = table.astype(BF16)
    rest = table - high.astype(F32)
    middle = rest.astype(BF16)
    low = (rest - middle.astype(F32)).astype(BF16)
    blocks = jnp.dot(jnp.concatenate([high, middle, low], axis=0), pick, preferred_element_type=F32)
    blocks = blocks[0:128] + blocks[128:256] + blocks[256:384]
    following = jnp.sum(jnp.where(lane, blocks, 0.0), axis=0, keepdims=True)

    live = 1.0 - terminal[...].reshape(1, 384).astype(F32)
    target = rewards[...].reshape(1, 384) + GAMMA * live * following
    weight = jnp.maximum(jnp.exp(advantage - top), FLOOR)
    miss_first, miss_second = first_q - target, second_q - target
    coeff = jnp.concatenate(
        [2.0 * miss_first, 2.0 * miss_second, -2.0 * expectile * advantage, -weight * scaled / sigma], axis=0
    )
    coeff = jnp.concatenate([jnp.where(mine, coeff, 0.0), jnp.zeros((5, 384), F32)], axis=0)
    high = coeff.astype(BF16)
    coeff = jnp.concatenate([high, (coeff - high.astype(F32)).astype(BF16)], axis=0)
    lanes = lax.broadcasted_iota(jnp.int32, (1, 128), 1)
    loss = jnp.zeros((1, 128), F32)
    for i, terms in enumerate((
        expectile * advantage * advantage, miss_first * miss_first + miss_second * miss_second, -weight * log_prob,
    )):
        loss = jnp.where(lanes == i, jnp.sum(terms, axis=1, keepdims=True), loss)
    loss = jnp.where(z == 6, loss, 0.0)
    last = lax.broadcasted_iota(jnp.int32, (16, 128), 0) == 15

    for j in range(8):
        g = jnp.dot(coeff, hid[j], preferred_element_type=F32)
        g = g[0:32] + g[32:64]
        for i in (0, 1):
            gb[2 * j + i, 0] = g[0:16, i * 128:(i + 1) * 128]
            gb[2 * j + i, 1] = jnp.where(last, loss, g[16:32, i * 128:(i + 1) * 128])
    copies = [send(gb.at[p[1], p[0]], rb.at[me], p) for p in plane]
    rb[me] = gb[row, d]
    wait_all(copies)
    zb[z] = jnp.sum(rb[...], axis=0)
    copies = [send(zb.at[z], zb.at[z], p) for p in line]
    wait_all(copies)
    ob[me] = jnp.concatenate([zb[0] + zb[2] + zb[4] + zb[6], zb[1] + zb[3] + zb[5] + zb[7]], axis=1)
    copies = [
        send(ob.at[me], ob.at[me], dev(d, (y + ky) % 4, (x + kx) % 4))
        for ky in range(4) for kx in range(4) if ky or kx
    ]
    wait_all(copies)
    both = ob.at[pl.ds(d * 16, 16)]
    copies = [send(both, both, dev(dd=1 - d))]
    wait_all(copies)
    total_rows = 384 * 32
    for s in range(16):
        grad_out[0:16, s * 256:(s + 1) * 256] = ob[s] * (1.0 / math.sqrt(total_rows))
        grad_out[16:27, s * 256:(s + 1) * 256] = ob[16 + s][0:11] * (1.0 / math.sqrt(total_rows))
    sums = ob[16][15:16, 0:128] * (1.0 / total_rows)
    for i in range(3):
        loss_out[i] = jnp.sum(jnp.where(lanes == i, sums, 0.0))
    drain(0)


N_COPIES = 14 + 14 + 48 + 48 + 16 + 8 + 31 + 31 + 7 + 15 + 1


def shards(states, actions, rewards, terminal, next_index, hidden_weights, action_weights, heads, policy_scale):
    vmem = pl.BlockSpec(memory_space=pltpu.VMEM)
    hbm = pl.BlockSpec(memory_space=pl.ANY)
    advantage, losses, grads = pl.pallas_call(
        update_kernel,
        out_shape=(
            jax.ShapeDtypeStruct((384,), F32),
            jax.ShapeDtypeStruct((3,), F32),
            jax.ShapeDtypeStruct((27, D), F32),
        ),
        in_specs=[hbm, hbm, hbm, hbm, hbm, vmem, vmem, vmem, vmem],
        out_specs=(vmem, pl.BlockSpec(memory_space=pltpu.SMEM), vmem),
        scratch_shapes=[
            pltpu.VMEM((8, 2, 4, 4, 128, 128), BF16),
            pltpu.VMEM((8, 2, 4, 4, 128, 128), BF16),
            pltpu.VMEM((8, 384, 512), BF16),
            pltpu.VMEM((8, 384, 256), F32),
            pltpu.VMEM((8, 384, 256), BF16),
            pltpu.VMEM((ACT, 384), BF16),
            pltpu.VMEM((2, ACT, D), BF16),
            pltpu.VMEM((27, D), BF16),
            pltpu.VMEM((8, 1, 384), F32),
            pltpu.VMEM((2, ACT, 384), F32),
            pltpu.VMEM((32, 8, 128), F32),
            pltpu.VMEM((16, 2, 16, 128), F32),
            pltpu.VMEM((32, 16, 128), F32),
            pltpu.VMEM((8, 16, 128), F32),
            pltpu.VMEM((32, 16, 256), F32),
            pltpu.SemaphoreType.DMA((6,)),
            pltpu.SemaphoreType.DMA((N_COPIES,)),
            pltpu.SemaphoreType.DMA((N_COPIES,)),
        ],
        compiler_params=pltpu.CompilerParams(
            collective_id=0, has_side_effects=True, vmem_limit_bytes=52 * 2**20
        ),
        name="update",
    )(states, hidden_weights, actions.T, action_weights, heads.T, rewards, terminal, next_index, policy_scale)
    return advantage, losses, grads.T


def solution(mesh):
    rows = P(("dp", "row"))
    return jax.shard_map(
        shards,
        mesh=mesh,
        in_specs=(P(("dp", "row"), "col"), P(("dp", "row"), None), rows, rows, rows, P(None, "col", "row"), P(), P(), P()),
        out_specs=(rows, P(), P()),
        check_vma=False,
    )
```

```python
import functools
import math

import jax
import jax.numpy as jnp
from jax import lax
from jax.experimental import pallas as pl
from jax.experimental.pallas import tpu as pltpu
from jax.sharding import PartitionSpec as P

D = 4096
ACT = 24
GAMMA = 0.99
TAU = 0.7
FLOOR = 0.01
MESH = pl.DeviceIdType.MESH
F32 = jnp.float32
BF16 = jnp.bfloat16

LAGS = (1, 2, 3)
UNROLL = 4
STATE_STEPS = (3, 5, 7)
PRODUCTS = {1: (0,), 3: (1, 7), 5: (2, 6)}

ORDER = (0, 1, 7, 2, 6, 3, 5, 4)


def place():
    row = lax.axis_index("row")
    return lax.axis_index("dp"), row // 4, row % 4, lax.axis_index("col")


def update_kernel(
    states, weights, act_hbm, act_w_hbm, heads_hbm, rewards, terminal, next_index, scale,
    adv_out, loss_out, grad_out,
    w_in, wa, wb, a, acc, hid, act_t, act_w, heads_t, qs, pol, vt, gb, rb, zb, ob, local_sem, ss, rs,
):
    d, y, x, z = place()
    net, half = z // 2, z % 2

    def dev(dd=None, yy=None, xx=None, zz=None):
        yy = y if yy is None else yy
        xx = x if xx is None else xx
        return (d if dd is None else dd, yy * 4 + xx, z if zz is None else zz)

    line = [dev(zz=(z + k) % 8) for k in range(1, 8)]
    plane = [
        dev((d + dd) % 2, (y + ky) % 4, (x + kx) % 4)
        for ky in range(4) for kx in range(4) for dd in range(2) if ky or kx or dd
    ]
    peers = line + plane

    held = pltpu.make_async_copy(weights, w_in, local_sem.at[0])
    held.start()
    own_states = pltpu.make_async_copy(states, a.at[z], local_sem.at[2])
    own_states.start()
    small = [
        pltpu.make_async_copy(src, dst, local_sem.at[3 + i])
        for i, (src, dst) in enumerate(((act_hbm, act_t), (act_w_hbm, act_w), (heads_hbm, heads_t)))
    ]
    for c in small:
        c.start()

    barrier = pltpu.get_barrier_semaphore()
    for p in peers:
        pl.semaphore_signal(barrier, inc=1, device_id=p, device_id_type=MESH)
    pl.semaphore_wait(barrier, len(peers))

    used = [0]
    sent = []

    def send(src, dst, device):
        i = used[0]
        used[0] += 1
        c = pltpu.make_async_remote_copy(
            src_ref=src, dst_ref=dst, send_sem=ss.at[i], recv_sem=rs.at[i],
            device_id=device, device_id_type=MESH,
        )
        c.start()
        sent.append(c)
        return c

    def drain(keep):
        while len(sent) > keep:
            sent.pop(0).wait_send()

    scatter = {}

    def scatter_weights(k):
        zt = (z + k) % 8
        cols = pl.ds(pl.multiple_of((zt % 2) * 128, 128), 128)
        scatter[(8 - k) % 8] = [
            send(
                w_in.at[zt // 2, pl.ds(pl.multiple_of(d * 256 + 128 * i, 128), 128), cols],
                dst, dev(zz=zt),
            )
            for i, dst in enumerate((wa.at[z, d, y, x], wb.at[z, d, x, y]))
        ]

    state_step = {}

    def send_states(t):
        copies = []
        for sign in (1, -1):
            c = (z - sign * (t - 1)) % 8
            pieces = (0, 1) if t < 4 else ((0,) if sign == 1 else (1,))
            for p in pieces:
                rows = pl.ds(p * 192, 192)
                src = states.at[rows] if t == 1 else a.at[c, rows]
                copies.append(send(src, a.at[c, rows], dev(zz=(z + sign) % 8)))
        state_step[t] = copies

    def wait_all(copies):
        for c in copies:
            c.wait_recv()

    first, second, third, swap = {}, {}, {}, {}

    def gather_first(r):
        wait_all(scatter.get(r, []))
        c = (z + r) % 8
        first[r] = []
        for k in (2, 1, 3):
            w = wa.at[c, d, y, x]
            first[r].append(send(w, w, dev(xx=(x + k) % 4)))
            w = wb.at[c, d, x, y]
            first[r].append(send(w, w, dev(yy=(y + k) % 4)))

    def gather_second(r):
        wait_all(first[r])
        c = (z + r) % 8
        second[r] = []
        for k in (1, 3):
            w = wa.at[c, d, y]
            second[r].append(send(w, w, dev(yy=(y + k) % 4)))
            w = wb.at[c, d, x]
            second[r].append(send(w, w, dev(xx=(x + k) % 4)))

    def gather_third(r):
        wait_all(second[r])
        c = (z + r) % 8
        third[r] = []
        for k in (1, 3):
            part = pl.ds(0 if k == 1 else 2, 2)
            w = wa.at[c, d, (y - k) % 4, part]
            third[r].append(send(w, w, dev(yy=(y + k) % 4)))
            w = wb.at[c, d, (x - k) % 4, part]
            third[r].append(send(w, w, dev(xx=(x + k) % 4)))
        swap[r] = []
        if r == ORDER[-1]:
            for k in (0, 1, 3):
                w = wa.at[c, d, (y + k) % 4]
                swap[r].append(send(w, w, dev(dd=1 - d)))
                w = wb.at[c, d, (x + k) % 4]
                swap[r].append(send(w, w, dev(dd=1 - d)))

    def exchange(r):
        wait_all(third[r])
        c = (z + r) % 8
        pair = (wa.at[c, d], wb.at[c, d])
        if r == ORDER[-1]:
            pair = (wa.at[c, d, (y + 2) % 4], wb.at[c, d, (x + 2) % 4])
        swap[r] += [send(w, w, dev(dd=1 - d)) for w in pair]

    def product(*group):
        chunks = [(z + r) % 8 for r in group]
        for r in group:
            wait_all(swap[r])

        def tile(j, _):
            yy, x0 = j // 2, 2 * (j % 2)
            rows = []
            for c in chunks:
                for dd in (0, 1):
                    rows.append(jnp.concatenate([wa[c, dd, yy, x0], wa[c, dd, yy, x0 + 1]], axis=1))
                    rows.append(jnp.concatenate([wb[c, dd, x0, yy], wb[c, dd, x0 + 1, yy]], axis=1))
            left = jnp.concatenate([a[c] for c in chunks], axis=1)
            acc[j] += jnp.dot(left, jnp.concatenate(rows, axis=0), preferred_element_type=F32)
            return 0

        lax.fori_loop(0, 8, tile, 0, unroll=UNROLL)

    held.wait()
    scatter_weights(1)
    scatter_weights(7)
    cols = pl.ds(pl.multiple_of(half * 128, 128), 128)
    wa[z, d, y, x] = w_in[net, pl.ds(pl.multiple_of(d * 256, 128), 128), cols]
    wb[z, d, x, y] = w_in[net, pl.ds(pl.multiple_of(d * 256 + 128, 128), 128), cols]
    gather_first(0)
    send_states(1)
    for k in (2, 6, 3, 5, 4):
        scatter_weights(k)

    weight_net = jnp.minimum(net, 1)
    gate = jnp.where(net < 2, 1.0, 0.0)

    def start_tile(j, _):
        cols = [
            act_w[weight_net, :, pl.ds(pl.multiple_of((2 * j + i) * 256 + half * 128, 128), 128)]
            for i in (0, 1)
        ]
        share = lax.dot_general(
            act_t[...], jnp.concatenate(cols, axis=1), (((0,), (0,)), ((), ())),
            preferred_element_type=F32,
        )
        acc[j] = share * gate
        return 0

    def start():
        for c in small:
            c.wait()
        lax.fori_loop(0, 8, start_tile, 0)
        own_states.wait()

    def pass_states(t):
        wait_all(state_step[t])
        if t < 4:
            send_states(t + 1)

    stages = ((gather_first, 0), (gather_second, LAGS[0]), (gather_third, LAGS[1]), (exchange, LAGS[2]))
    for step in range(8 + LAGS[2]):
        for stage, lag in stages:
            i = step - lag
            if 0 <= i < 8 and step > 0:
                stage(ORDER[i])
        for t in range(1, 4):
            if step == STATE_STEPS[t - 1]:
                pass_states(t)
        if step == 1:
            start()
        if step - LAGS[2] in PRODUCTS:
            product(*PRODUCTS[step - LAGS[2]])
        drain(80)
    product(3, 5)
    pass_states(4)
    product(4)

    total = jnp.zeros((27, 384), F32)
    for j in range(8):
        h = jnp.maximum(acc[j], 0.0).astype(BF16)
        hid[j] = h
        cols = [
            heads_t[:, pl.ds(pl.multiple_of((2 * j + i) * 256 + half * 128, 128), 128)]
            for i in (0, 1)
        ]
        total += lax.dot_general(
            jnp.concatenate(cols, axis=1), h, (((1,), (1,)), ((), ())),
            preferred_element_type=F32,
        )
    mine = jnp.minimum(lax.broadcasted_iota(jnp.int32, (27, 384), 0), 3) == net
    part = jnp.where(mine, total, 0.0)

    row = y * 4 + x
    me = d * 16 + row
    qs[z] = jnp.sum(part[0:3], axis=0, keepdims=True)
    pol[0] = part[3:27]
    copies = [send(pol.at[0], pol.at[1], dev(zz=z + 1 - 2 * half))]
    copies += [send(qs.at[z], qs.at[z], p) for p in line]
    index = next_index[...].reshape(1, 384)
    r = lax.broadcasted_iota(jnp.int32, (256, 384), 0)
    block = jnp.where((r & 7) < 3, (r >> 3) * 3 + (r & 7), -1)
    pick = jnp.where(block == (index >> 7), 1.0, 0.0).astype(BF16)
    lane = lax.broadcasted_iota(jnp.int32, (128, 384), 0) == (index & 127)
    eye = lax.broadcasted_iota(jnp.int32, (24, 24), 0) == lax.broadcasted_iota(jnp.int32, (24, 24), 1)
    sigma = jnp.sum(jnp.where(eye, scale[...].reshape(1, 24), 0.0), axis=1, keepdims=True)
    wait_all(copies)
    first_q, second_q, value = qs[0] + qs[1], qs[2] + qs[3], qs[4] + qs[5]
    policy_mean = pol[0] + pol[1]
    advantage = jnp.minimum(first_q, second_q) - value
    vt[me] = jnp.concatenate(
        [value[:, 0:128], value[:, 128:256], value[:, 256:384],
         jnp.broadcast_to(jnp.max(advantage, axis=1, keepdims=True), (1, 128)), jnp.zeros((4, 128), F32)],
        axis=0,
    )
    copies = [send(vt.at[me], vt.at[me], p) for p in plane]
    adv_out[...] = advantage.reshape(384)
    expectile = jnp.where(advantage >= 0.0, TAU, 1.0 - TAU)
    scaled = (act_t[...].astype(F32) - policy_mean) / sigma
    log_prob = -0.5 * jnp.sum(scaled * scaled, axis=0, keepdims=True)
    wait_all(copies)

    table = vt[...].reshape(256, 128)
    fourth = (lax.broadcasted_iota(jnp.int32, (256, 128), 0) & 7) == 3
    top = jnp.max(jnp.where(fourth, table, -jnp.inf), keepdims=True)
    table = table.T
    high = table.astype(BF16)
    rest = table - high.astype(F32)
    middle = rest.astype(BF16)
    low = (rest - middle.astype(F32)).astype(BF16)
    blocks = jnp.dot(jnp.concatenate([high, middle, low], axis=0), pick, preferred_element_type=F32)
    blocks = blocks[0:128] + blocks[128:256] + blocks[256:384]
    following = jnp.sum(jnp.where(lane, blocks, 0.0), axis=0, keepdims=True)

    live = 1.0 - terminal[...].reshape(1, 384).astype(F32)
    target = rewards[...].reshape(1, 384) + GAMMA * live * following
    weight = jnp.maximum(jnp.exp(advantage - top), FLOOR)
    miss_first, miss_second = first_q - target, second_q - target
    coeff = jnp.concatenate(
        [2.0 * miss_first, 2.0 * miss_second, -2.0 * expectile * advantage, -weight * scaled / sigma], axis=0
    )
    coeff = jnp.concatenate([jnp.where(mine, coeff, 0.0), jnp.zeros((5, 384), F32)], axis=0)
    high = coeff.astype(BF16)
    coeff = jnp.concatenate([high, (coeff - high.astype(F32)).astype(BF16)], axis=0)
    lanes = lax.broadcasted_iota(jnp.int32, (1, 128), 1)
    loss = jnp.zeros((1, 128), F32)
    for i, terms in enumerate((
        expectile * advantage * advantage, miss_first * miss_first + miss_second * miss_second, -weight * log_prob,
    )):
        loss = jnp.where(lanes == i, jnp.sum(terms, axis=1, keepdims=True), loss)
    loss = jnp.where(z == 6, loss, 0.0)
    last = lax.broadcasted_iota(jnp.int32, (16, 128), 0) == 15

    for j in range(8):
        g = jnp.dot(coeff, hid[j], preferred_element_type=F32)
        g = g[0:32] + g[32:64]
        for i in (0, 1):
            gb[2 * j + i, 0] = g[0:16, i * 128:(i + 1) * 128]
            gb[2 * j + i, 1] = jnp.where(last, loss, g[16:32, i * 128:(i + 1) * 128])
    copies = [send(gb.at[p[1], p[0]], rb.at[me], p) for p in plane]
    rb[me] = gb[row, d]
    wait_all(copies)
    zb[z] = jnp.sum(rb[...], axis=0)
    copies = [send(zb.at[z], zb.at[z], p) for p in line]
    wait_all(copies)
    ob[me] = jnp.concatenate([zb[0] + zb[2] + zb[4] + zb[6], zb[1] + zb[3] + zb[5] + zb[7]], axis=1)
    copies = [
        send(ob.at[me], ob.at[me], dev(d, (y + ky) % 4, (x + kx) % 4))
        for ky in range(4) for kx in range(4) if ky or kx
    ]
    wait_all(copies)
    both = ob.at[pl.ds(d * 16, 16)]
    copies = [send(both, both, dev(dd=1 - d))]
    wait_all(copies)
    total_rows = 384 * 32
    for s in range(16):
        grad_out[0:16, s * 256:(s + 1) * 256] = ob[s] * (1.0 / math.sqrt(total_rows))
        grad_out[16:27, s * 256:(s + 1) * 256] = ob[16 + s][0:11] * (1.0 / math.sqrt(total_rows))
    sums = ob[16][15:16, 0:128] * (1.0 / total_rows)
    for i in range(3):
        loss_out[i] = jnp.sum(jnp.where(lanes == i, sums, 0.0))
    drain(0)


N_COPIES = 14 + 14 + 48 + 32 + 32 + 22 + 8 + 31 + 31 + 7 + 15 + 1


def shards(states, actions, rewards, terminal, next_index, hidden_weights, action_weights, heads, policy_scale):
    vmem = pl.BlockSpec(memory_space=pltpu.VMEM)
    hbm = pl.BlockSpec(memory_space=pltpu.HBM)
    advantage, losses, grads = pl.pallas_call(
        update_kernel,
        out_shape=(
            jax.ShapeDtypeStruct((384,), F32),
            jax.ShapeDtypeStruct((3,), F32),
            jax.ShapeDtypeStruct((27, D), F32),
        ),
        in_specs=[hbm, hbm, hbm, hbm, hbm, vmem, vmem, vmem, vmem],
        out_specs=(vmem, pl.BlockSpec(memory_space=pltpu.SMEM), vmem),
        scratch_shapes=[
            pltpu.VMEM((4, 512, 256), BF16),
            pltpu.VMEM((8, 2, 4, 4, 128, 128), BF16),
            pltpu.VMEM((8, 2, 4, 4, 128, 128), BF16),
            pltpu.VMEM((8, 384, 512), BF16),
            pltpu.VMEM((8, 384, 256), F32),
            pltpu.VMEM((8, 384, 256), BF16),
            pltpu.VMEM((ACT, 384), BF16),
            pltpu.VMEM((2, ACT, D), BF16),
            pltpu.VMEM((27, D), BF16),
            pltpu.VMEM((8, 1, 384), F32),
            pltpu.VMEM((2, ACT, 384), F32),
            pltpu.VMEM((32, 8, 128), F32),
            pltpu.VMEM((16, 2, 16, 128), F32),
            pltpu.VMEM((32, 16, 128), F32),
            pltpu.VMEM((8, 16, 128), F32),
            pltpu.VMEM((32, 16, 256), F32),
            pltpu.SemaphoreType.DMA((6,)),
            pltpu.SemaphoreType.DMA((N_COPIES,)),
            pltpu.SemaphoreType.DMA((N_COPIES,)),
        ],
        compiler_params=pltpu.CompilerParams(
            collective_id=0, has_side_effects=True, vmem_limit_bytes=60 * 2**20
        ),
        name="update",
    )(states, hidden_weights, actions.T, action_weights, heads.T, rewards, terminal, next_index, policy_scale)
    return advantage, losses, grads.T


def solution(mesh):
    rows = P(("dp", "row"))
    return jax.shard_map(
        shards,
        mesh=mesh,
        in_specs=(P(("dp", "row"), "col"), P(("dp", "row"), None), rows, rows, rows, P(None, "col", "row"), P(), P(), P()),
        out_specs=(rows, P(), P()),
        check_vma=False,
    )
```

```python
import functools
import math

import jax
import jax.numpy as jnp
from jax import lax
from jax.experimental import pallas as pl
from jax.experimental.pallas import tpu as pltpu
from jax.sharding import PartitionSpec as P

D = 4096
ACT = 24
GAMMA = 0.99
TAU = 0.7
FLOOR = 0.01
MESH = pl.DeviceIdType.MESH
F32 = jnp.float32
BF16 = jnp.bfloat16

LAGS = (1, 2, 3)
UNROLL = 4
STATE_STEPS = (3, 5, 7)
PRODUCTS = {1: (0,), 3: (1, 7), 5: (2, 6)}

ORDER = (0, 1, 7, 2, 6, 3, 5, 4)


def place():
    row = lax.axis_index("row")
    return lax.axis_index("dp"), row // 4, row % 4, lax.axis_index("col")


def update_kernel(
    states, weights, act_hbm, act_w_hbm, heads_hbm, rewards, terminal, next_index, scale,
    adv_out, loss_out, grad_out,
    w_in, wa, wb, a, acc, hid, act_t, act_w, heads_t, qs, pol, vt, gb, rb, zb, ob, local_sem, ss, rs,
):
    d, y, x, z = place()
    net, half = z // 2, z % 2

    def dev(dd=None, yy=None, xx=None, zz=None):
        yy = y if yy is None else yy
        xx = x if xx is None else xx
        return (d if dd is None else dd, yy * 4 + xx, z if zz is None else zz)

    line = [dev(zz=(z + k) % 8) for k in (4, 3, 5, 2, 6, 1, 7)]
    plane = {
        ky: [
            dev((d + dd) % 2, (y + ky) % 4, (x + kx) % 4)
            for kx in (2, 1, 3, 0) for dd in range(2) if ky or kx or dd
        ]
        for ky in (2, 1, 3, 0)
    }
    rows_of_plane, plane = plane, sum(plane.values(), [])
    peers = line + plane

    held = pltpu.make_async_copy(weights, w_in, local_sem.at[0])
    held.start()
    own_states = pltpu.make_async_copy(states, a.at[z], local_sem.at[2])
    own_states.start()
    small = [
        pltpu.make_async_copy(src, dst, local_sem.at[3 + i])
        for i, (src, dst) in enumerate(((act_hbm, act_t), (act_w_hbm, act_w), (heads_hbm, heads_t)))
    ]
    for c in small:
        c.start()

    barrier = pltpu.get_barrier_semaphore()
    for p in peers:
        pl.semaphore_signal(barrier, inc=1, device_id=p, device_id_type=MESH)
    pl.semaphore_wait(barrier, len(peers))

    used = [0]
    sent = []

    def send(src, dst, device):
        i = used[0]
        used[0] += 1
        c = pltpu.make_async_remote_copy(
            src_ref=src, dst_ref=dst, send_sem=ss.at[i], recv_sem=rs.at[i],
            device_id=device, device_id_type=MESH,
        )
        c.start()
        sent.append(c)
        return c

    def drain(keep):
        while len(sent) > keep:
            sent.pop(0).wait_send()

    scatter = {}

    def scatter_weights(k):
        zt = (z + k) % 8
        cols = pl.ds(pl.multiple_of((zt % 2) * 128, 128), 128)
        scatter[(8 - k) % 8] = [
            send(
                w_in.at[zt // 2, pl.ds(pl.multiple_of(d * 256 + 128 * i, 128), 128), cols],
                dst, dev(zz=zt),
            )
            for i, dst in enumerate((wa.at[z, d, y, x], wb.at[z, d, x, y]))
        ]

    state_step = {}

    def send_states(t):
        copies = []
        for sign in (1, -1):
            c = (z - sign * (t - 1)) % 8
            pieces = (0, 1) if t < 4 else ((0,) if sign == 1 else (1,))
            for p in pieces:
                rows = pl.ds(p * 192, 192)
                src = states.at[rows] if t == 1 else a.at[c, rows]
                copies.append(send(src, a.at[c, rows], dev(zz=(z + sign) % 8)))
        state_step[t] = copies

    def wait_all(copies):
        for c in copies:
            c.wait_recv()

    first, second, third, swap = {}, {}, {}, {}

    def gather_first(r):
        wait_all(scatter.get(r, []))
        c = (z + r) % 8
        first[r] = []
        for k in (2, 1, 3):
            w = wa.at[c, d, y, x]
            first[r].append(send(w, w, dev(xx=(x + k) % 4)))
            w = wb.at[c, d, x, y]
            first[r].append(send(w, w, dev(yy=(y + k) % 4)))

    def gather_second(r):
        wait_all(first[r])
        c = (z + r) % 8
        second[r] = []
        for k in (1, 3):
            w = wa.at[c, d, y]
            second[r].append(send(w, w, dev(yy=(y + k) % 4)))
            w = wb.at[c, d, x]
            second[r].append(send(w, w, dev(xx=(x + k) % 4)))

    def gather_third(r):
        wait_all(second[r])
        c = (z + r) % 8
        third[r] = []
        for k in (1, 3):
            part = pl.ds(0 if k == 1 else 2, 2)
            w = wa.at[c, d, (y - k) % 4, part]
            third[r].append(send(w, w, dev(yy=(y + k) % 4)))
            w = wb.at[c, d, (x - k) % 4, part]
            third[r].append(send(w, w, dev(xx=(x + k) % 4)))
        swap[r] = []
        if r == ORDER[-1]:
            for k in (0, 1, 3):
                w = wa.at[c, d, (y + k) % 4]
                swap[r].append(send(w, w, dev(dd=1 - d)))
                w = wb.at[c, d, (x + k) % 4]
                swap[r].append(send(w, w, dev(dd=1 - d)))

    def exchange(r):
        wait_all(third[r])
        c = (z + r) % 8
        pair = (wa.at[c, d], wb.at[c, d])
        if r == ORDER[-1]:
            pair = (wa.at[c, d, (y + 2) % 4], wb.at[c, d, (x + 2) % 4])
        swap[r] += [send(w, w, dev(dd=1 - d)) for w in pair]

    def product(*group):
        chunks = [(z + r) % 8 for r in group]
        for r in group:
            wait_all(swap[r])

        def tile(j, _):
            yy, x0 = j // 2, 2 * (j % 2)
            rows = []
            for c in chunks:
                for dd in (0, 1):
                    rows.append(jnp.concatenate([wa[c, dd, yy, x0], wa[c, dd, yy, x0 + 1]], axis=1))
                    rows.append(jnp.concatenate([wb[c, dd, x0, yy], wb[c, dd, x0 + 1, yy]], axis=1))
            left = jnp.concatenate([a[c] for c in chunks], axis=1)
            acc[j] += jnp.dot(left, jnp.concatenate(rows, axis=0), preferred_element_type=F32)
            return 0

        lax.fori_loop(0, 8, tile, 0, unroll=UNROLL)

    held.wait()
    scatter_weights(1)
    scatter_weights(7)
    cols = pl.ds(pl.multiple_of(half * 128, 128), 128)
    wa[z, d, y, x] = w_in[net, pl.ds(pl.multiple_of(d * 256, 128), 128), cols]
    wb[z, d, x, y] = w_in[net, pl.ds(pl.multiple_of(d * 256 + 128, 128), 128), cols]
    gather_first(0)
    send_states(1)
    for k in (2, 6, 3, 5, 4):
        scatter_weights(k)

    weight_net = jnp.minimum(net, 1)
    gate = jnp.where(net < 2, 1.0, 0.0)

    def start_tile(j, _):
        cols = [
            act_w[weight_net, :, pl.ds(pl.multiple_of((2 * j + i) * 256 + half * 128, 128), 128)]
            for i in (0, 1)
        ]
        share = lax.dot_general(
            act_t[...], jnp.concatenate(cols, axis=1), (((0,), (0,)), ((), ())),
            preferred_element_type=F32,
        )
        acc[j] = share * gate
        return 0

    def start():
        for c in small:
            c.wait()
        lax.fori_loop(0, 8, start_tile, 0)
        own_states.wait()

    def pass_states(t):
        wait_all(state_step[t])
        if t < 4:
            send_states(t + 1)

    stages = ((gather_first, 0), (gather_second, LAGS[0]), (gather_third, LAGS[1]), (exchange, LAGS[2]))
    for step in range(8 + LAGS[2]):
        for stage, lag in stages:
            i = step - lag
            if 0 <= i < 8 and step > 0:
                stage(ORDER[i])
        for t in range(1, 4):
            if step == STATE_STEPS[t - 1]:
                pass_states(t)
        if step == 1:
            start()
        if step - LAGS[2] in PRODUCTS:
            product(*PRODUCTS[step - LAGS[2]])
        drain(80)
    product(3, 5)
    pass_states(4)
    product(4)

    total = jnp.zeros((27, 384), F32)
    for j in range(8):
        h = jnp.maximum(acc[j], 0.0).astype(BF16)
        hid[j] = h
        cols = [
            heads_t[:, pl.ds(pl.multiple_of((2 * j + i) * 256 + half * 128, 128), 128)]
            for i in (0, 1)
        ]
        total += lax.dot_general(
            jnp.concatenate(cols, axis=1), h, (((1,), (1,)), ((), ())),
            preferred_element_type=F32,
        )
    mine = jnp.minimum(lax.broadcasted_iota(jnp.int32, (27, 384), 0), 3) == net
    part = jnp.where(mine, total, 0.0)

    row = y * 4 + x
    me = d * 16 + row
    qs[z] = jnp.sum(part[0:3], axis=0, keepdims=True)
    pol[0] = part[3:27]
    copies = [send(pol.at[0], pol.at[1], dev(zz=z + 1 - 2 * half))]
    copies += [send(qs.at[z], qs.at[z], p) for p in line]
    index = next_index[...].reshape(1, 384)
    r = lax.broadcasted_iota(jnp.int32, (256, 384), 0)
    block = jnp.where((r & 7) < 3, (r >> 3) * 3 + (r & 7), -1)
    pick = jnp.where(block == (index >> 7), 1.0, 0.0).astype(BF16)
    lane = lax.broadcasted_iota(jnp.int32, (128, 384), 0) == (index & 127)
    eye = lax.broadcasted_iota(jnp.int32, (24, 24), 0) == lax.broadcasted_iota(jnp.int32, (24, 24), 1)
    sigma = jnp.sum(jnp.where(eye, scale[...].reshape(1, 24), 0.0), axis=1, keepdims=True)
    wait_all(copies)
    first_q, second_q, value = qs[0] + qs[1], qs[2] + qs[3], qs[4] + qs[5]
    policy_mean = pol[0] + pol[1]
    advantage = jnp.minimum(first_q, second_q) - value
    vt[me] = jnp.concatenate(
        [value[:, 0:128], value[:, 128:256], value[:, 256:384],
         jnp.broadcast_to(jnp.max(advantage, axis=1, keepdims=True), (1, 128)), jnp.zeros((4, 128), F32)],
        axis=0,
    )
    mark = used[0]
    copies = [send(vt.at[me], vt.at[me], p) for p in plane]
    adv_out[...] = advantage.reshape(384)
    expectile = jnp.where(advantage >= 0.0, TAU, 1.0 - TAU)
    scaled = (act_t[...].astype(F32) - policy_mean) / sigma
    log_prob = -0.5 * jnp.sum(scaled * scaled, axis=0, keepdims=True)
    wait_all(copies)

    table = vt[...].reshape(256, 128)
    fourth = (lax.broadcasted_iota(jnp.int32, (256, 128), 0) & 7) == 3
    top = jnp.max(jnp.where(fourth, table, -jnp.inf), keepdims=True)
    table = table.T
    high = table.astype(BF16)
    rest = table - high.astype(F32)
    middle = rest.astype(BF16)
    low = (rest - middle.astype(F32)).astype(BF16)
    blocks = jnp.dot(jnp.concatenate([high, middle, low], axis=0), pick, preferred_element_type=F32)
    blocks = blocks[0:128] + blocks[128:256] + blocks[256:384]
    following = jnp.sum(jnp.where(lane, blocks, 0.0), axis=0, keepdims=True)

    live = 1.0 - terminal[...].reshape(1, 384).astype(F32)
    target = rewards[...].reshape(1, 384) + GAMMA * live * following
    weight = jnp.maximum(jnp.exp(advantage - top), FLOOR)
    miss_first, miss_second = first_q - target, second_q - target
    coeff = jnp.concatenate(
        [2.0 * miss_first, 2.0 * miss_second, -2.0 * expectile * advantage, -weight * scaled / sigma], axis=0
    )
    coeff = jnp.concatenate([jnp.where(mine, coeff, 0.0), jnp.zeros((5, 384), F32)], axis=0)
    high = coeff.astype(BF16)
    coeff = jnp.concatenate([high, (coeff - high.astype(F32)).astype(BF16)], axis=0)
    lanes = lax.broadcasted_iota(jnp.int32, (1, 128), 1)
    loss = jnp.zeros((1, 128), F32)
    for i, terms in enumerate((
        expectile * advantage * advantage, miss_first * miss_first + miss_second * miss_second, -weight * log_prob,
    )):
        loss = jnp.where(lanes == i, jnp.sum(terms, axis=1, keepdims=True), loss)
    loss = jnp.where(z == 6, loss, 0.0)
    last = lax.broadcasted_iota(jnp.int32, (16, 128), 0) == 15

    copies = []
    for ky in (2, 1, 3, 0):
        for j in range(2):
            tile_at = 2 * ((y + ky) % 4) + j
            g = jnp.dot(coeff, hid[tile_at], preferred_element_type=F32)
            g = g[0:32] + g[32:64]
            for i in (0, 1):
                gb[2 * tile_at + i, 0] = g[0:16, i * 128:(i + 1) * 128]
                gb[2 * tile_at + i, 1] = jnp.where(last, loss, g[16:32, i * 128:(i + 1) * 128])
        copies += [send(gb.at[p[1], p[0]], rb.at[me], p) for p in rows_of_plane[ky]]
    rb[me] = gb[row, d]
    wait_all(copies)

    total_rows = 384 * 32
    sums = jnp.sum(rb[...], axis=0)
    bottom = d == 1
    loss_row = sums[15:16] * (1.0 / total_rows)
    loss_high = loss_row.astype(BF16).astype(F32)
    sums = sums * (1.0 / math.sqrt(total_rows))
    at_row = lax.broadcasted_iota(jnp.int32, (16, 128), 0)
    with_loss = jnp.where(at_row == 15, loss_high, jnp.where(at_row == 14, loss_row - loss_high, sums))
    zb[z] = jnp.where(bottom, with_loss, sums).astype(BF16)
    copies = [send(zb.at[z], zb.at[z], p) for p in line]
    drain(7)
    wait_all(copies)
    pair = [
        zb[i].astype(F32) + zb[2 + i].astype(F32) + zb[4 + i].astype(F32) + zb[6 + i].astype(F32) for i in (0, 1)
    ]
    ob[me] = jnp.concatenate(pair, axis=1).astype(BF16)
    used[0] = mark
    copies = [send(ob.at[me], ob.at[me], p) for p in plane]
    wait_all(copies)
    for s in range(16):
        grad_out[0:16, s * 256:(s + 1) * 256] = ob[s].astype(F32)
        grad_out[16:27, s * 256:(s + 1) * 256] = ob[16 + s].astype(F32)[0:11]
    sums = ob[16].astype(F32)
    sums = sums[14:15, 0:128] + sums[15:16, 0:128]
    for i in range(3):
        loss_out[i] = jnp.sum(jnp.where(lanes == i, sums, 0.0))
    drain(0)


N_COPIES = 14 + 14 + 48 + 32 + 32 + 22 + 8 + 31 + 31 + 7


def shards(states, actions, rewards, terminal, next_index, hidden_weights, action_weights, heads, policy_scale):
    vmem = pl.BlockSpec(memory_space=pltpu.VMEM)
    hbm = pl.BlockSpec(memory_space=pltpu.HBM)
    advantage, losses, grads = pl.pallas_call(
        update_kernel,
        out_shape=(
            jax.ShapeDtypeStruct((384,), F32),
            jax.ShapeDtypeStruct((3,), F32),
            jax.ShapeDtypeStruct((27, D), F32),
        ),
        in_specs=[hbm, hbm, hbm, hbm, hbm, vmem, vmem, vmem, vmem],
        out_specs=(vmem, pl.BlockSpec(memory_space=pltpu.SMEM), vmem),
        scratch_shapes=[
            pltpu.VMEM((4, 512, 256), BF16),
            pltpu.VMEM((8, 2, 4, 4, 128, 128), BF16),
            pltpu.VMEM((8, 2, 4, 4, 128, 128), BF16),
            pltpu.VMEM((8, 384, 512), BF16),
            pltpu.VMEM((8, 384, 256), F32),
            pltpu.VMEM((8, 384, 256), BF16),
            pltpu.VMEM((ACT, 384), BF16),
            pltpu.VMEM((2, ACT, D), BF16),
            pltpu.VMEM((27, D), BF16),
            pltpu.VMEM((8, 1, 384), F32),
            pltpu.VMEM((2, ACT, 384), F32),
            pltpu.VMEM((32, 8, 128), F32),
            pltpu.VMEM((16, 2, 16, 128), F32),
            pltpu.VMEM((32, 16, 128), F32),
            pltpu.VMEM((8, 16, 128), BF16),
            pltpu.VMEM((32, 16, 256), BF16),
            pltpu.SemaphoreType.DMA((6,)),
            pltpu.SemaphoreType.DMA((N_COPIES,)),
            pltpu.SemaphoreType.DMA((N_COPIES,)),
        ],
        compiler_params=pltpu.CompilerParams(
            collective_id=0, has_side_effects=True, vmem_limit_bytes=40 * 2**20
        ),
        name="update",
    )(
        *(pltpu.with_memory_space_constraint(v, pltpu.HBM)
          for v in (states, hidden_weights, actions.T, action_weights, heads.T)),
        rewards, terminal, next_index, policy_scale,
    )
    return advantage, losses, grads.T


def solution(mesh):
    rows = P(("dp", "row"))
    return jax.shard_map(
        shards,
        mesh=mesh,
        in_specs=(P(("dp", "row"), "col"), P(("dp", "row"), None), rows, rows, rows, P(None, "col", "row"), P(), P(), P()),
        out_specs=(rows, P(), P()),
        check_vma=False,
    )
```

```python
import functools
import math

import jax
import jax.numpy as jnp
from jax import lax
from jax.experimental import pallas as pl
from jax.experimental.pallas import tpu as pltpu
from jax.sharding import PartitionSpec as P

D = 4096
ACT = 24
GAMMA = 0.99
TAU = 0.7
FLOOR = 0.01
MESH = pl.DeviceIdType.MESH
F32 = jnp.float32
BF16 = jnp.bfloat16

LAGS = (1, 2, 3)
UNROLL = 4
STATE_STEPS = (4, 6, 8)
PRODUCTS = {1: (0,), 3: (1, 7), 5: (2, 6)}

ORDER = (0, 1, 7, 2, 6, 3, 5, 4)


def place():
    row = lax.axis_index("row")
    return lax.axis_index("dp"), row // 4, row % 4, lax.axis_index("col")


def update_kernel(
    states, weights, act_hbm, act_w_hbm, heads_hbm, rewards, terminal, next_index, scale,
    adv_out, loss_out, grad_out,
    w_in, wa, wb, a, acc, hid, act_t, act_w, heads_t, qs, pol, vt, gb, rb, zb, ob, local_sem, ss, rs,
):
    d, y, x, z = place()
    net, half = z // 2, z % 2

    def dev(dd=None, yy=None, xx=None, zz=None):
        yy = y if yy is None else yy
        xx = x if xx is None else xx
        return (d if dd is None else dd, yy * 4 + xx, z if zz is None else zz)

    line = [dev(zz=(z + k) % 8) for k in (4, 3, 5, 2, 6, 1, 7)]
    plane = {
        ky: [
            dev((d + dd) % 2, (y + ky) % 4, (x + kx) % 4)
            for kx in (2, 1, 3, 0) for dd in range(2) if ky or kx or dd
        ]
        for ky in (2, 1, 3, 0)
    }
    rows_of_plane, plane = plane, sum(plane.values(), [])
    peers = line + [dev(xx=(x + k) % 4) for k in (2, 1, 3)] + [dev(yy=(y + k) % 4) for k in (2, 1, 3)] + [dev(dd=1 - d)]

    held = pltpu.make_async_copy(weights, w_in, local_sem.at[0])
    held.start()
    own_states = pltpu.make_async_copy(states, a.at[z], local_sem.at[2])
    own_states.start()
    small = [
        pltpu.make_async_copy(src, dst, local_sem.at[3 + i])
        for i, (src, dst) in enumerate(((act_hbm, act_t), (act_w_hbm, act_w), (heads_hbm, heads_t)))
    ]
    for c in small:
        c.start()

    barrier = pltpu.get_barrier_semaphore()
    for p in peers:
        pl.semaphore_signal(barrier, inc=1, device_id=p, device_id_type=MESH)
    pl.semaphore_wait(barrier, len(peers))

    used = [0]
    sent = []

    def send(src, dst, device):
        i = used[0]
        used[0] += 1
        c = pltpu.make_async_remote_copy(
            src_ref=src, dst_ref=dst, send_sem=ss.at[i], recv_sem=rs.at[i],
            device_id=device, device_id_type=MESH,
        )
        c.start()
        sent.append(c)
        return c

    def drain(keep):
        while len(sent) > keep:
            sent.pop(0).wait_send()

    scatter = {}

    def scatter_weights(k):
        zt = (z + k) % 8
        cols = pl.ds(pl.multiple_of((zt % 2) * 128, 128), 128)
        scatter[(8 - k) % 8] = [
            send(
                w_in.at[zt // 2, pl.ds(pl.multiple_of(d * 256 + 128 * i, 128), 128), cols],
                dst, dev(zz=zt),
            )
            for i, dst in enumerate((wa.at[z, d, y, x], wb.at[z, d, x, y]))
        ]

    state_step = {}

    def send_states(t):
        copies = []
        for sign in (1, -1):
            c = (z - sign * (t - 1)) % 8
            pieces = (0, 1) if t < 4 else ((0,) if sign == 1 else (1,))
            for p in pieces:
                rows = pl.ds(p * 192, 192)
                src = states.at[rows] if t == 1 else a.at[c, rows]
                copies.append(send(src, a.at[c, rows], dev(zz=(z + sign) % 8)))
        state_step[t] = copies

    def wait_all(copies):
        for c in copies:
            c.wait_recv()

    first, second, third, swap = {}, {}, {}, {}

    def gather_first(r):
        wait_all(scatter.get(r, []))
        c = (z + r) % 8
        first[r] = []
        for k in (2, 1, 3):
            w = wa.at[c, d, y, x]
            first[r].append(send(w, w, dev(xx=(x + k) % 4)))
            w = wb.at[c, d, x, y]
            first[r].append(send(w, w, dev(yy=(y + k) % 4)))

    def gather_second(r):
        wait_all(first[r])
        c = (z + r) % 8
        second[r] = []
        for k in (1, 3):
            w = wa.at[c, d, y]
            second[r].append(send(w, w, dev(yy=(y + k) % 4)))
            w = wb.at[c, d, x]
            second[r].append(send(w, w, dev(xx=(x + k) % 4)))

    def gather_third(r):
        wait_all(second[r])
        c = (z + r) % 8
        third[r] = []
        for k in (1, 3):
            part = pl.ds(0 if k == 1 else 2, 2)
            w = wa.at[c, d, (y - k) % 4, part]
            third[r].append(send(w, w, dev(yy=(y + k) % 4)))
            w = wb.at[c, d, (x - k) % 4, part]
            third[r].append(send(w, w, dev(xx=(x + k) % 4)))
        swap[r] = []
        if r == ORDER[-1]:
            for k in (0, 1, 3):
                w = wa.at[c, d, (y + k) % 4]
                swap[r].append(send(w, w, dev(dd=1 - d)))
                w = wb.at[c, d, (x + k) % 4]
                swap[r].append(send(w, w, dev(dd=1 - d)))

    def exchange(r):
        wait_all(third[r])
        c = (z + r) % 8
        pair = (wa.at[c, d], wb.at[c, d])
        if r == ORDER[-1]:
            pair = (wa.at[c, d, (y + 2) % 4], wb.at[c, d, (x + 2) % 4])
        swap[r] += [send(w, w, dev(dd=1 - d)) for w in pair]

    def product(*group):
        chunks = [(z + r) % 8 for r in group]
        for r in group:
            wait_all(swap[r])

        def tile(j, _):
            yy, x0 = j // 2, 2 * (j % 2)
            rows = []
            for c in chunks:
                for dd in (0, 1):
                    rows.append(jnp.concatenate([wa[c, dd, yy, x0], wa[c, dd, yy, x0 + 1]], axis=1))
                    rows.append(jnp.concatenate([wb[c, dd, x0, yy], wb[c, dd, x0 + 1, yy]], axis=1))
            left = jnp.concatenate([a[c] for c in chunks], axis=1)
            acc[j] += jnp.dot(left, jnp.concatenate(rows, axis=0), preferred_element_type=F32)
            return 0

        lax.fori_loop(0, 8, tile, 0, unroll=UNROLL)

    held.wait()
    scatter_weights(1)
    scatter_weights(7)
    cols = pl.ds(pl.multiple_of(half * 128, 128), 128)
    wa[z, d, y, x] = w_in[net, pl.ds(pl.multiple_of(d * 256, 128), 128), cols]
    wb[z, d, x, y] = w_in[net, pl.ds(pl.multiple_of(d * 256 + 128, 128), 128), cols]
    gather_first(0)
    send_states(1)
    for k in (2, 6, 3, 5, 4):
        scatter_weights(k)

    weight_net = jnp.minimum(net, 1)
    gate = jnp.where(net < 2, 1.0, 0.0)

    def start_tile(j, _):
        cols = [
            act_w[weight_net, :, pl.ds(pl.multiple_of((2 * j + i) * 256 + half * 128, 128), 128)]
            for i in (0, 1)
        ]
        share = lax.dot_general(
            act_t[...], jnp.concatenate(cols, axis=1), (((0,), (0,)), ((), ())),
            preferred_element_type=F32,
        )
        acc[j] = share * gate
        return 0

    def start():
        for c in small:
            c.wait()
        lax.fori_loop(0, 8, start_tile, 0)
        own_states.wait()

    def pass_states(t):
        wait_all(state_step[t])
        if t < 4:
            send_states(t + 1)

    stages = ((gather_first, 0), (gather_second, LAGS[0]), (gather_third, LAGS[1]), (exchange, LAGS[2]))
    for step in range(8 + LAGS[2]):
        for stage, lag in stages:
            i = step - lag
            if 0 <= i < 8 and step > 0:
                stage(ORDER[i])
        for t in range(1, 4):
            if step == STATE_STEPS[t - 1]:
                pass_states(t)
        if step == 1:
            start()
        if step - LAGS[2] in PRODUCTS:
            product(*PRODUCTS[step - LAGS[2]])
        drain(80)
    product(3, 5)
    pass_states(4)
    product(4)

    total = jnp.zeros((27, 384), F32)
    for j in range(8):
        h = jnp.maximum(acc[j], 0.0).astype(BF16)
        hid[j] = h
        cols = [
            heads_t[:, pl.ds(pl.multiple_of((2 * j + i) * 256 + half * 128, 128), 128)]
            for i in (0, 1)
        ]
        total += lax.dot_general(
            jnp.concatenate(cols, axis=1), h, (((1,), (1,)), ((), ())),
            preferred_element_type=F32,
        )
    mine = jnp.minimum(lax.broadcasted_iota(jnp.int32, (27, 384), 0), 3) == net
    part = jnp.where(mine, total, 0.0)

    row = y * 4 + x
    me = d * 16 + row
    qs[z] = jnp.sum(part[0:3], axis=0, keepdims=True)
    pol[0] = part[3:27]
    copies = [send(pol.at[0], pol.at[1], dev(zz=z + 1 - 2 * half))]
    copies += [send(qs.at[z], qs.at[z], p) for p in line]
    index = next_index[...].reshape(1, 384)
    r = lax.broadcasted_iota(jnp.int32, (256, 384), 0)
    block = jnp.where((r & 7) < 3, (r >> 3) * 3 + (r & 7), -1)
    pick = jnp.where(block == (index >> 7), 1.0, 0.0).astype(BF16)
    lane = lax.broadcasted_iota(jnp.int32, (128, 384), 0) == (index & 127)
    eye = lax.broadcasted_iota(jnp.int32, (24, 24), 0) == lax.broadcasted_iota(jnp.int32, (24, 24), 1)
    sigma = jnp.sum(jnp.where(eye, scale[...].reshape(1, 24), 0.0), axis=1, keepdims=True)
    wait_all(copies)
    first_q, second_q, value = qs[0] + qs[1], qs[2] + qs[3], qs[4] + qs[5]
    policy_mean = pol[0] + pol[1]
    advantage = jnp.minimum(first_q, second_q) - value
    vt[me] = jnp.concatenate(
        [value[:, 0:128], value[:, 128:256], value[:, 256:384],
         jnp.broadcast_to(jnp.max(advantage, axis=1, keepdims=True), (1, 128)), jnp.zeros((4, 128), F32)],
        axis=0,
    )
    mark = used[0]
    copies = [send(vt.at[me], vt.at[me], p) for p in plane]
    adv_out[...] = advantage.reshape(384)
    expectile = jnp.where(advantage >= 0.0, TAU, 1.0 - TAU)
    scaled = (act_t[...].astype(F32) - policy_mean) / sigma
    log_prob = -0.5 * jnp.sum(scaled * scaled, axis=0, keepdims=True)
    wait_all(copies)

    table = vt[...].reshape(256, 128)
    fourth = (lax.broadcasted_iota(jnp.int32, (256, 128), 0) & 7) == 3
    top = jnp.max(jnp.where(fourth, table, -jnp.inf), keepdims=True)
    table = table.T
    high = table.astype(BF16)
    rest = table - high.astype(F32)
    middle = rest.astype(BF16)
    low = (rest - middle.astype(F32)).astype(BF16)
    blocks = jnp.dot(jnp.concatenate([high, middle, low], axis=0), pick, preferred_element_type=F32)
    blocks = blocks[0:128] + blocks[128:256] + blocks[256:384]
    following = jnp.sum(jnp.where(lane, blocks, 0.0), axis=0, keepdims=True)

    live = 1.0 - terminal[...].reshape(1, 384).astype(F32)
    target = rewards[...].reshape(1, 384) + GAMMA * live * following
    weight = jnp.maximum(jnp.exp(advantage - top), FLOOR)
    miss_first, miss_second = first_q - target, second_q - target
    coeff = jnp.concatenate(
        [2.0 * miss_first, 2.0 * miss_second, -2.0 * expectile * advantage, -weight * scaled / sigma], axis=0
    )
    coeff = jnp.concatenate([jnp.where(mine, coeff, 0.0), jnp.zeros((5, 384), F32)], axis=0)
    high = coeff.astype(BF16)
    coeff = jnp.concatenate([high, (coeff - high.astype(F32)).astype(BF16)], axis=0)
    lanes = lax.broadcasted_iota(jnp.int32, (1, 128), 1)
    loss = jnp.zeros((1, 128), F32)
    for i, terms in enumerate((
        expectile * advantage * advantage, miss_first * miss_first + miss_second * miss_second, -weight * log_prob,
    )):
        loss = jnp.where(lanes == i, jnp.sum(terms, axis=1, keepdims=True), loss)
    loss = jnp.where(z == 6, loss, 0.0)
    last = lax.broadcasted_iota(jnp.int32, (16, 128), 0) == 15

    copies = []
    for ky in (2, 1, 3, 0):
        for j in range(2):
            tile_at = 2 * ((y + ky) % 4) + j
            g = jnp.dot(coeff, hid[tile_at], preferred_element_type=F32)
            g = g[0:32] + g[32:64]
            for i in (0, 1):
                gb[2 * tile_at + i, 0] = g[0:16, i * 128:(i + 1) * 128]
                gb[2 * tile_at + i, 1] = jnp.where(last, loss, g[16:32, i * 128:(i + 1) * 128])
        copies += [send(gb.at[p[1], p[0]], rb.at[me], p) for p in rows_of_plane[ky]]
    rb[me] = gb[row, d]
    wait_all(copies)

    total_rows = 384 * 32
    sums = jnp.sum(rb[...], axis=0)
    bottom = d == 1
    loss_row = sums[15:16] * (1.0 / total_rows)
    loss_high = loss_row.astype(BF16).astype(F32)
    sums = sums * (1.0 / math.sqrt(total_rows))
    at_row = lax.broadcasted_iota(jnp.int32, (16, 128), 0)
    with_loss = jnp.where(at_row == 15, loss_high, jnp.where(at_row == 14, loss_row - loss_high, sums))
    zb[z] = jnp.where(bottom, with_loss, sums).astype(BF16)
    copies = [send(zb.at[z], zb.at[z], p) for p in line]
    drain(7)
    wait_all(copies)
    pair = [
        zb[i].astype(F32) + zb[2 + i].astype(F32) + zb[4 + i].astype(F32) + zb[6 + i].astype(F32) for i in (0, 1)
    ]
    ob[me] = jnp.concatenate(pair, axis=1).astype(BF16)
    used[0] = mark
    copies = [send(ob.at[me], ob.at[me], p) for p in plane]
    wait_all(copies)
    for s in range(16):
        grad_out[0:16, s * 256:(s + 1) * 256] = ob[s].astype(F32)
        grad_out[16:27, s * 256:(s + 1) * 256] = ob[16 + s].astype(F32)[0:11]
    sums = ob[16].astype(F32)
    sums = sums[14:15, 0:128] + sums[15:16, 0:128]
    for i in range(3):
        loss_out[i] = jnp.sum(jnp.where(lanes == i, sums, 0.0))
    drain(0)


N_COPIES = 14 + 14 + 48 + 32 + 32 + 22 + 8 + 31 + 31 + 7


def shards(states, actions, rewards, terminal, next_index, hidden_weights, action_weights, heads, policy_scale):
    vmem = pl.BlockSpec(memory_space=pltpu.VMEM)
    hbm = pl.BlockSpec(memory_space=pltpu.HBM)
    advantage, losses, grads = pl.pallas_call(
        update_kernel,
        out_shape=(
            jax.ShapeDtypeStruct((384,), F32),
            jax.ShapeDtypeStruct((3,), F32),
            jax.ShapeDtypeStruct((27, D), F32),
        ),
        in_specs=[hbm, hbm, hbm, hbm, hbm, vmem, vmem, vmem, vmem],
        out_specs=(vmem, pl.BlockSpec(memory_space=pltpu.SMEM), vmem),
        scratch_shapes=[
            pltpu.VMEM((4, 512, 256), BF16),
            pltpu.VMEM((8, 2, 4, 4, 128, 128), BF16),
            pltpu.VMEM((8, 2, 4, 4, 128, 128), BF16),
            pltpu.VMEM((8, 384, 512), BF16),
            pltpu.VMEM((8, 384, 256), F32),
            pltpu.VMEM((8, 384, 256), BF16),
            pltpu.VMEM((ACT, 384), BF16),
            pltpu.VMEM((2, ACT, D), BF16),
            pltpu.VMEM((27, D), BF16),
            pltpu.VMEM((8, 1, 384), F32),
            pltpu.VMEM((2, ACT, 384), F32),
            pltpu.VMEM((32, 8, 128), F32),
            pltpu.VMEM((16, 2, 16, 128), F32),
            pltpu.VMEM((32, 16, 128), F32),
            pltpu.VMEM((8, 16, 128), BF16),
            pltpu.VMEM((32, 16, 256), BF16),
            pltpu.SemaphoreType.DMA((6,)),
            pltpu.SemaphoreType.DMA((N_COPIES,)),
            pltpu.SemaphoreType.DMA((N_COPIES,)),
        ],
        compiler_params=pltpu.CompilerParams(
            collective_id=0, has_side_effects=True, vmem_limit_bytes=40 * 2**20
        ),
        name="update",
    )(
        *(pltpu.with_memory_space_constraint(v, pltpu.HBM)
          for v in (states, hidden_weights, actions.T, action_weights, heads.T)),
        rewards, terminal, next_index, policy_scale,
    )
    return advantage, losses, grads.T


def solution(mesh):
    rows = P(("dp", "row"))
    return jax.shard_map(
        shards,
        mesh=mesh,
        in_specs=(P(("dp", "row"), "col"), P(("dp", "row"), None), rows, rows, rows, P(None, "col", "row"), P(), P(), P()),
        out_specs=(rows, P(), P()),
        check_vma=False,
    )
```

```python
import functools
import math

import jax
import jax.numpy as jnp
from jax import lax
from jax.experimental import pallas as pl
from jax.experimental.pallas import tpu as pltpu
from jax.sharding import PartitionSpec as P

D = 4096
ACT = 24
GAMMA = 0.99
TAU = 0.7
FLOOR = 0.01
MESH = pl.DeviceIdType.MESH
F32 = jnp.float32
BF16 = jnp.bfloat16

LAGS = (1, 2, 3)
UNROLL = 4
STATE_STEPS = (4, 7, 9)
PRODUCTS = {1: (0,), 3: (1, 7), 5: (2, 6)}

ORDER = (0, 1, 7, 2, 6, 3, 5, 4)


def place():
    row = lax.axis_index("row")
    return lax.axis_index("dp"), row // 4, row % 4, lax.axis_index("col")


def update_kernel(
    states, weights, act_hbm, act_w_hbm, heads_hbm, rewards, terminal, next_index, scale,
    adv_out, loss_out, grad_out,
    w_in, wa, wb, a, acc, hid, act_t, act_w, heads_t, qs, pol, vt, gb, rb, zb, ob, local_sem, ss, rs,
):
    d, y, x, z = place()
    net, half = z // 2, z % 2

    def dev(dd=None, yy=None, xx=None, zz=None):
        yy = y if yy is None else yy
        xx = x if xx is None else xx
        return (d if dd is None else dd, yy * 4 + xx, z if zz is None else zz)

    line = [dev(zz=(z + k) % 8) for k in (4, 3, 5, 2, 6, 1, 7)]
    plane = {
        ky: [
            dev((d + dd) % 2, (y + ky) % 4, (x + kx) % 4)
            for kx in (2, 1, 3, 0) for dd in range(2) if ky or kx or dd
        ]
        for ky in (2, 1, 3, 0)
    }
    rows_of_plane, plane = plane, sum(plane.values(), [])
    peers = line + [dev(xx=(x + k) % 4) for k in (2, 1, 3)] + [dev(yy=(y + k) % 4) for k in (2, 1, 3)] + [dev(dd=1 - d)]

    held = pltpu.make_async_copy(weights, w_in, local_sem.at[0])
    held.start()
    own_states = pltpu.make_async_copy(states, a.at[z], local_sem.at[2])
    own_states.start()
    small = [
        pltpu.make_async_copy(src, dst, local_sem.at[3 + i])
        for i, (src, dst) in enumerate(((act_hbm, act_t), (act_w_hbm, act_w), (heads_hbm, heads_t)))
    ]
    for c in small:
        c.start()

    barrier = pltpu.get_barrier_semaphore()
    for p in peers:
        pl.semaphore_signal(barrier, inc=1, device_id=p, device_id_type=MESH)
    pl.semaphore_wait(barrier, len(peers))

    used = [0]
    sent = []

    def send(src, dst, device):
        i = used[0]
        used[0] += 1
        c = pltpu.make_async_remote_copy(
            src_ref=src, dst_ref=dst, send_sem=ss.at[i], recv_sem=rs.at[i],
            device_id=device, device_id_type=MESH,
        )
        c.start()
        sent.append(c)
        return c

    def drain(keep):
        while len(sent) > keep:
            sent.pop(0).wait_send()

    scatter = {}

    def scatter_weights(k):
        zt = (z + k) % 8
        cols = pl.ds(pl.multiple_of((zt % 2) * 128, 128), 128)
        scatter[(8 - k) % 8] = [
            send(
                w_in.at[zt // 2, pl.ds(pl.multiple_of(d * 256 + 128 * i, 128), 128), cols],
                dst, dev(zz=zt),
            )
            for i, dst in enumerate((wa.at[z, d, y, x], wb.at[z, d, x, y]))
        ]

    state_step = {}

    def send_states(t):
        copies = []
        for sign in (1, -1):
            c = (z - sign * (t - 1)) % 8
            pieces = (0, 1) if t < 4 else ((0,) if sign == 1 else (1,))
            for p in pieces:
                rows = pl.ds(p * 192, 192)
                src = states.at[rows] if t == 1 else a.at[c, rows]
                copies.append(send(src, a.at[c, rows], dev(zz=(z + sign) % 8)))
        state_step[t] = copies

    def wait_all(copies):
        for c in copies:
            c.wait_recv()

    first, second, third, swap = {}, {}, {}, {}

    def gather_first(r):
        wait_all(scatter.get(r, []))
        c = (z + r) % 8
        first[r] = []
        for k in (2, 1, 3):
            w = wa.at[c, d, y, x]
            first[r].append(send(w, w, dev(xx=(x + k) % 4)))
            w = wb.at[c, d, x, y]
            first[r].append(send(w, w, dev(yy=(y + k) % 4)))

    def gather_second(r):
        wait_all(first[r])
        c = (z + r) % 8
        second[r] = []
        for k in (1, 3):
            w = wa.at[c, d, y]
            second[r].append(send(w, w, dev(yy=(y + k) % 4)))
            w = wb.at[c, d, x]
            second[r].append(send(w, w, dev(xx=(x + k) % 4)))

    def gather_third(r):
        wait_all(second[r])
        c = (z + r) % 8
        third[r] = []
        for k in (1, 3):
            part = pl.ds(0 if k == 1 else 2, 2)
            w = wa.at[c, d, (y - k) % 4, part]
            third[r].append(send(w, w, dev(yy=(y + k) % 4)))
            w = wb.at[c, d, (x - k) % 4, part]
            third[r].append(send(w, w, dev(xx=(x + k) % 4)))
        swap[r] = []
        if r == ORDER[-1]:
            for k in (0, 1, 3):
                w = wa.at[c, d, (y + k) % 4]
                swap[r].append(send(w, w, dev(dd=1 - d)))
                w = wb.at[c, d, (x + k) % 4]
                swap[r].append(send(w, w, dev(dd=1 - d)))

    def exchange(r):
        wait_all(third[r])
        c = (z + r) % 8
        pair = (wa.at[c, d], wb.at[c, d])
        if r == ORDER[-1]:
            pair = (wa.at[c, d, (y + 2) % 4], wb.at[c, d, (x + 2) % 4])
        swap[r] += [send(w, w, dev(dd=1 - d)) for w in pair]

    def product(*group):
        chunks = [(z + r) % 8 for r in group]
        for r in group:
            wait_all(swap[r])

        def tile(j, _):
            yy, x0 = j // 2, 2 * (j % 2)
            rows = []
            for c in chunks:
                for dd in (0, 1):
                    rows.append(jnp.concatenate([wa[c, dd, yy, x0], wa[c, dd, yy, x0 + 1]], axis=1))
                    rows.append(jnp.concatenate([wb[c, dd, x0, yy], wb[c, dd, x0 + 1, yy]], axis=1))
            left = jnp.concatenate([a[c] for c in chunks], axis=1)
            acc[j] += jnp.dot(left, jnp.concatenate(rows, axis=0), preferred_element_type=F32)
            return 0

        lax.fori_loop(0, 8, tile, 0, unroll=UNROLL)

    held.wait()
    scatter_weights(1)
    scatter_weights(7)
    cols = pl.ds(pl.multiple_of(half * 128, 128), 128)
    wa[z, d, y, x] = w_in[net, pl.ds(pl.multiple_of(d * 256, 128), 128), cols]
    wb[z, d, x, y] = w_in[net, pl.ds(pl.multiple_of(d * 256 + 128, 128), 128), cols]
    gather_first(0)
    send_states(1)
    for k in (2, 6, 3, 5, 4):
        scatter_weights(k)

    weight_net = jnp.minimum(net, 1)
    gate = jnp.where(net < 2, 1.0, 0.0)

    def start_tile(j, _):
        cols = [
            act_w[weight_net, :, pl.ds(pl.multiple_of((2 * j + i) * 256 + half * 128, 128), 128)]
            for i in (0, 1)
        ]
        share = lax.dot_general(
            act_t[...], jnp.concatenate(cols, axis=1), (((0,), (0,)), ((), ())),
            preferred_element_type=F32,
        )
        acc[j] = share * gate
        return 0

    def start():
        for c in small:
            c.wait()
        lax.fori_loop(0, 8, start_tile, 0)
        own_states.wait()

    def pass_states(t):
        wait_all(state_step[t])
        if t < 4:
            send_states(t + 1)

    stages = ((gather_first, 0), (gather_second, LAGS[0]), (gather_third, LAGS[1]), (exchange, LAGS[2]))
    for step in range(8 + LAGS[2]):
        for stage, lag in stages:
            i = step - lag
            if 0 <= i < 8 and step > 0:
                stage(ORDER[i])
        for t in range(1, 4):
            if step == STATE_STEPS[t - 1]:
                pass_states(t)
        if step == 1:
            start()
        if step - LAGS[2] in PRODUCTS:
            product(*PRODUCTS[step - LAGS[2]])
        drain(80)
    product(3, 5)
    pass_states(4)
    product(4)

    total = jnp.zeros((27, 384), F32)
    for j in range(8):
        h = jnp.maximum(acc[j], 0.0).astype(BF16)
        hid[j] = h
        cols = [
            heads_t[:, pl.ds(pl.multiple_of((2 * j + i) * 256 + half * 128, 128), 128)]
            for i in (0, 1)
        ]
        total += lax.dot_general(
            jnp.concatenate(cols, axis=1), h, (((1,), (1,)), ((), ())),
            preferred_element_type=F32,
        )
    mine = jnp.minimum(lax.broadcasted_iota(jnp.int32, (27, 384), 0), 3) == net
    part = jnp.where(mine, total, 0.0)

    row = y * 4 + x
    me = d * 16 + row
    qs[z] = jnp.sum(part[0:3], axis=0, keepdims=True)
    pol[0] = part[3:27]
    copies = [send(pol.at[0], pol.at[1], dev(zz=z + 1 - 2 * half))]
    copies += [send(qs.at[z], qs.at[z], p) for p in line]
    index = next_index[...].reshape(1, 384)
    r = lax.broadcasted_iota(jnp.int32, (256, 384), 0)
    block = jnp.where((r & 7) < 3, (r >> 3) * 3 + (r & 7), -1)
    pick = jnp.where(block == (index >> 7), 1.0, 0.0).astype(BF16)
    lane = lax.broadcasted_iota(jnp.int32, (128, 384), 0) == (index & 127)
    eye = lax.broadcasted_iota(jnp.int32, (24, 24), 0) == lax.broadcasted_iota(jnp.int32, (24, 24), 1)
    sigma = jnp.sum(jnp.where(eye, scale[...].reshape(1, 24), 0.0), axis=1, keepdims=True)
    wait_all(copies)
    first_q, second_q, value = qs[0] + qs[1], qs[2] + qs[3], qs[4] + qs[5]
    policy_mean = pol[0] + pol[1]
    advantage = jnp.minimum(first_q, second_q) - value
    vt[me] = jnp.concatenate(
        [value[:, 0:128], value[:, 128:256], value[:, 256:384],
         jnp.broadcast_to(jnp.max(advantage, axis=1, keepdims=True), (1, 128)), jnp.zeros((4, 128), F32)],
        axis=0,
    )
    mark = used[0]
    copies = [send(vt.at[me], vt.at[me], p) for p in plane]
    adv_out[...] = advantage.reshape(384)
    expectile = jnp.where(advantage >= 0.0, TAU, 1.0 - TAU)
    scaled = (act_t[...].astype(F32) - policy_mean) / sigma
    log_prob = -0.5 * jnp.sum(scaled * scaled, axis=0, keepdims=True)
    wait_all(copies)

    table = vt[...].reshape(256, 128)
    fourth = (lax.broadcasted_iota(jnp.int32, (256, 128), 0) & 7) == 3
    top = jnp.max(jnp.where(fourth, table, -jnp.inf), keepdims=True)
    table = table.T
    high = table.astype(BF16)
    rest = table - high.astype(F32)
    middle = rest.astype(BF16)
    low = (rest - middle.astype(F32)).astype(BF16)
    blocks = jnp.dot(jnp.concatenate([high, middle, low], axis=0), pick, preferred_element_type=F32)
    blocks = blocks[0:128] + blocks[128:256] + blocks[256:384]
    following = jnp.sum(jnp.where(lane, blocks, 0.0), axis=0, keepdims=True)

    live = 1.0 - terminal[...].reshape(1, 384).astype(F32)
    target = rewards[...].reshape(1, 384) + GAMMA * live * following
    weight = jnp.maximum(jnp.exp(advantage - top), FLOOR)
    miss_first, miss_second = first_q - target, second_q - target
    coeff = jnp.concatenate(
        [2.0 * miss_first, 2.0 * miss_second, -2.0 * expectile * advantage, -weight * scaled / sigma], axis=0
    )
    coeff = jnp.concatenate([jnp.where(mine, coeff, 0.0), jnp.zeros((5, 384), F32)], axis=0)
    high = coeff.astype(BF16)
    coeff = jnp.concatenate([high, (coeff - high.astype(F32)).astype(BF16)], axis=0)
    lanes = lax.broadcasted_iota(jnp.int32, (1, 128), 1)
    loss = jnp.zeros((1, 128), F32)
    for i, terms in enumerate((
        expectile * advantage * advantage, miss_first * miss_first + miss_second * miss_second, -weight * log_prob,
    )):
        loss = jnp.where(lanes == i, jnp.sum(terms, axis=1, keepdims=True), loss)
    loss = jnp.where(z == 6, loss, 0.0)
    last = lax.broadcasted_iota(jnp.int32, (16, 128), 0) == 15

    copies = []
    for ky in (2, 1, 3, 0):
        for j in range(2):
            tile_at = 2 * ((y + ky) % 4) + j
            g = jnp.dot(coeff, hid[tile_at], preferred_element_type=F32)
            g = g[0:32] + g[32:64]
            for i in (0, 1):
                gb[2 * tile_at + i, 0] = g[0:16, i * 128:(i + 1) * 128]
                gb[2 * tile_at + i, 1] = jnp.where(last, loss, g[16:32, i * 128:(i + 1) * 128])
        copies += [send(gb.at[p[1], p[0]], rb.at[me], p) for p in rows_of_plane[ky]]
    rb[me] = gb[row, d]
    wait_all(copies)

    total_rows = 384 * 32
    sums = jnp.sum(rb[...], axis=0)
    bottom = d == 1
    loss_row = sums[15:16] * (1.0 / total_rows)
    loss_high = loss_row.astype(BF16).astype(F32)
    sums = sums * (1.0 / math.sqrt(total_rows))
    at_row = lax.broadcasted_iota(jnp.int32, (16, 128), 0)
    with_loss = jnp.where(at_row == 15, loss_high, jnp.where(at_row == 14, loss_row - loss_high, sums))
    zb[z] = jnp.where(bottom, with_loss, sums).astype(BF16)
    copies = [send(zb.at[z], zb.at[z], p) for p in line]
    drain(7)
    wait_all(copies)
    pair = [
        zb[i].astype(F32) + zb[2 + i].astype(F32) + zb[4 + i].astype(F32) + zb[6 + i].astype(F32) for i in (0, 1)
    ]
    ob[me] = jnp.concatenate(pair, axis=1).astype(BF16)
    used[0] = mark
    copies = [send(ob.at[me], ob.at[me], p) for p in plane]
    drain(0)
    wait_all(copies)
    for s in range(16):
        grad_out[0:16, s * 256:(s + 1) * 256] = ob[s].astype(F32)
        grad_out[16:27, s * 256:(s + 1) * 256] = ob[16 + s].astype(F32)[0:11]
    sums = ob[16].astype(F32)
    sums = sums[14:15, 0:128] + sums[15:16, 0:128]
    for i in range(3):
        loss_out[i] = jnp.sum(jnp.where(lanes == i, sums, 0.0))
    drain(0)


N_COPIES = 14 + 14 + 48 + 32 + 32 + 22 + 8 + 31 + 31 + 7


def shards(states, actions, rewards, terminal, next_index, hidden_weights, action_weights, heads, policy_scale):
    vmem = pl.BlockSpec(memory_space=pltpu.VMEM)
    hbm = pl.BlockSpec(memory_space=pltpu.HBM)
    advantage, losses, grads = pl.pallas_call(
        update_kernel,
        out_shape=(
            jax.ShapeDtypeStruct((384,), F32),
            jax.ShapeDtypeStruct((3,), F32),
            jax.ShapeDtypeStruct((27, D), F32),
        ),
        in_specs=[hbm, hbm, hbm, hbm, hbm, vmem, vmem, vmem, vmem],
        out_specs=(vmem, pl.BlockSpec(memory_space=pltpu.SMEM), vmem),
        scratch_shapes=[
            pltpu.VMEM((4, 512, 256), BF16),
            pltpu.VMEM((8, 2, 4, 4, 128, 128), BF16),
            pltpu.VMEM((8, 2, 4, 4, 128, 128), BF16),
            pltpu.VMEM((8, 384, 512), BF16),
            pltpu.VMEM((8, 384, 256), F32),
            pltpu.VMEM((8, 384, 256), BF16),
            pltpu.VMEM((ACT, 384), BF16),
            pltpu.VMEM((2, ACT, D), BF16),
            pltpu.VMEM((27, D), BF16),
            pltpu.VMEM((8, 1, 384), F32),
            pltpu.VMEM((2, ACT, 384), F32),
            pltpu.VMEM((32, 8, 128), F32),
            pltpu.VMEM((16, 2, 16, 128), F32),
            pltpu.VMEM((32, 16, 128), F32),
            pltpu.VMEM((8, 16, 128), BF16),
            pltpu.VMEM((32, 16, 256), BF16),
            pltpu.SemaphoreType.DMA((6,)),
            pltpu.SemaphoreType.DMA((N_COPIES,)),
            pltpu.SemaphoreType.DMA((N_COPIES,)),
        ],
        compiler_params=pltpu.CompilerParams(
            collective_id=0, has_side_effects=True, vmem_limit_bytes=40 * 2**20
        ),
        name="update",
    )(
        *(pltpu.with_memory_space_constraint(v, pltpu.HBM)
          for v in (states, hidden_weights, actions.T, action_weights, heads.T)),
        rewards, terminal, next_index, policy_scale,
    )
    return advantage, losses, grads.T


def solution(mesh):
    rows = P(("dp", "row"))
    return jax.shard_map(
        shards,
        mesh=mesh,
        in_specs=(P(("dp", "row"), "col"), P(("dp", "row"), None), rows, rows, rows, P(None, "col", "row"), P(), P(), P()),
        out_specs=(rows, P(), P()),
        check_vma=False,
    )
```
